256 devices in a mesh: grp: 8 (over z_lo, core), dev: 32 (over y, z_hi, x).
Axes of the slice: x: 4, y: 4, z: 8 (z_hi: 2, z_lo: 4; z = z_hi * 4 + z_lo), core: 2. Of those that a mesh axis runs over, the one named last changes fastest.
Arguments:
- features: bfloat16 [8, 512, 128, 256], P('grp', 'dev'), may hold values from -6 to 6
- offsets: float32 [8, 512, 3, 128], P('grp', 'dev'), may hold values from 0 to 1
- radial: bfloat16 [8, 512, 8, 128, 128], P('grp', 'dev'), may hold values from -0.25 to 0.25
- neighbours: int32 [8, 512, 8], P('grp', 'dev'), may hold values from 0 to 8, as said below
- counts: int32 [8, 512], P('grp', 'dev'), may hold values from 16 to 128
- wavevectors: int32 [3, 1024], replicated, may hold values from -8 to 8
- w_msg: bfloat16 [256, 256], replicated, may hold values from -0.375 to 0.375
- w_mix: bfloat16 [256, 256], replicated, may hold values from -0.375 to 0.375
Outputs:
- updated: bfloat16 [8, 512, 128, 256], P('grp', 'dev')
The draws below stay inside these ranges and needn't reach their ends.
Inputs may be any that keep to these rules, and one draw needn't show every extreme that they name: `neighbours`: A cell's 8 codes are distinct; code c names the cell at (c // 3 - 1) slabs and (c % 3 - 1) cells away along the slab.
All inputs are finite; a program needn't handle non-finite values.
Results may differ from the reference program's by a relative error of at most 0.018.
Values may be sent and summed in bfloat16 or wider, within the bound.
A program may use at most 128 MiB of HBM per device.

```python
import math
import jax
import jax.numpy as jnp
from jax import lax

CHANNELS = 256
WAVES = 1024
ATOMS = 128
PAIRS = 8
GRID_Z = 8
CELL_LINE = 512
TOTAL_SLOTS = 524288


def draw_neighbours(key, part):
    scores = jax.random.randint(key, (GRID_Z, CELL_LINE, 9), 0, 1 << 20) * 16 + jnp.arange(9, dtype=jnp.int32)
    values, picked = lax.top_k(scores, PAIRS)
    return picked.astype(jnp.int32)


def set_ends(values, rng, least, largest):
    dims = values.shape
    place = [jax.random.randint(jax.random.fold_in(rng, axis), (), 0, dims[axis]) for axis in range(len(dims))]
    values = values.at[tuple(place)].set(least)
    longest = dims.index(max(dims))
    place[longest] = (place[longest] + 1) % dims[longest]
    return values.at[tuple(place)].set(largest)


def block_levels(own_key, shape, split, smallest, largest):
    def one(dim, shards_of):
        draws = jax.random.uniform(jax.random.fold_in(jax.random.fold_in(own_key, 6), dim), (shards_of,), jnp.float32, smallest / len(split), largest / len(split))
        return jnp.repeat(jnp.exp(draws), shape[dim] // shards_of).reshape((-1,) + (1,) * (len(shape) - dim - 1))

    gain = one(*split[0])
    for cut in split[1:]:
        gain = gain * one(*cut)
    return gain


def gaussian(own_key, extent, spread, most, shards=(), held_as=jnp.bfloat16):
    drawn = spread * jax.random.normal(own_key, extent, jnp.float32)
    if shards:
        drawn = drawn * block_levels(own_key, extent, shards, -0.22, 0.18)
    return jnp.clip(drawn, -most, most).astype(held_as)


def setup_inputs(seed: int = 0) -> dict:
    seeds = jax.random.split(jax.random.key(seed), 9)
    features = gaussian(seeds[0], (GRID_Z, CELL_LINE, ATOMS, CHANNELS), 1.0, 6.0, ((0, 8), (1, 32)))
    offsets = jnp.clip(1.0 * jax.random.uniform(seeds[1], (GRID_Z, CELL_LINE, 3, ATOMS), jnp.float32) ** block_levels(seeds[1], (GRID_Z, CELL_LINE, 3, ATOMS), ((0, 8), (1, 32)), -0.2, 0.2), 0.0, 1.0)
    radial = gaussian(seeds[2], (GRID_Z, CELL_LINE, PAIRS, ATOMS, ATOMS), (ATOMS * PAIRS // 2) ** -0.5, 0.25, ((0, 8), (1, 32)))
    neighbours = draw_neighbours(jax.random.fold_in(seeds[8], 71), 0)
    counts = set_ends(jax.random.randint(seeds[4], (GRID_Z, CELL_LINE), ATOMS // 8, ATOMS + 1), jax.random.fold_in(seeds[4], 1), ATOMS // 8, ATOMS).astype(jnp.int32)
    wavevectors = set_ends(jax.random.randint(seeds[5], (3, WAVES), -8, 9), jax.random.fold_in(seeds[5], 1), -8, 8).astype(jnp.int32)
    w_msg = gaussian(seeds[6], (CHANNELS, CHANNELS), CHANNELS ** -0.5, 0.375)
    w_mix = gaussian(seeds[7], (CHANNELS, CHANNELS), CHANNELS ** -0.5, 0.375)
    return {"features": features, "offsets": offsets, "radial": radial, "neighbours": neighbours, "counts": counts, "wavevectors": wavevectors, "w_msg": w_msg, "w_mix": w_mix}


def wave_kernel(wavevectors):
    waves = wavevectors.astype(jnp.float32)
    square = lax.optimization_barrier(jnp.sum(waves * waves, axis=0))
    kernel = jnp.exp(-square / 128.0) / (1.0 + square / 64.0)
    return jnp.concatenate([kernel, kernel])

def trig_rows(offsets, group, wavevectors):
    waves = wavevectors.astype(jnp.float32)
    cell_pos = jnp.arange(CELL_LINE, dtype=jnp.int32).astype(jnp.float32)
    along_x = (cell_pos[:, None] + offsets[:, 0, :]) / CELL_LINE
    along_y = offsets[:, 1, :]
    along_z = (group.astype(jnp.float32) + offsets[:, 2, :]) / GRID_Z
    phase = 2.0 * math.pi * (along_x[..., None] * waves[0] + along_y[..., None] * waves[1] + along_z[..., None] * waves[2])
    table = jnp.concatenate([jnp.cos(phase), jnp.sin(phase)], axis=-1).astype(jnp.bfloat16)
    return table.reshape(CELL_LINE * ATOMS, 2 * WAVES)

def reference(features, offsets, radial, neighbours, counts, wavevectors, w_msg, w_mix):
    slot_ids = jnp.arange(ATOMS, dtype=jnp.int32)
    masking = (slot_ids[None, None, :] < counts[:, :, None]).astype(jnp.bfloat16)
    masked = features * masking[..., None]
    padded = jnp.pad(masked, ((1, 1), (1, 1), (0, 0), (0, 0)))
    cell_ids = jnp.arange(CELL_LINE, dtype=jnp.int32)
    groups = jnp.arange(GRID_Z, dtype=jnp.int32)

    def short_group(group):
        window = lax.dynamic_slice_in_dim(padded, group, 3, 0)
        codes = neighbours[group]
        blocks = radial[group]
        total = jnp.zeros((CELL_LINE, ATOMS, CHANNELS), jnp.float32)
        for neighbour in range(PAIRS):
            code = codes[:, neighbour]
            picked = window[code // 3, cell_ids + code % 3]
            total = total + jnp.einsum('kab,kbc->kac', blocks[:, neighbour].astype(jnp.float32), picked.astype(jnp.float32))
        return total
    gathered = lax.map(short_group, groups)

    def factor_group(group):
        table = trig_rows(offsets[group], group, wavevectors)
        return lax.dot_general(table, masked[group].reshape(CELL_LINE * ATOMS, CHANNELS), (((0,), (0,)), ((), ())), preferred_element_type=jnp.float32)
    sums = lax.optimization_barrier(jnp.sum(lax.map(factor_group, groups), axis=0))
    factors = (sums * (1.0 / math.sqrt(TOTAL_SLOTS))).astype(jnp.bfloat16)
    energy = (jnp.dot(factors, w_mix, preferred_element_type=jnp.float32) * wave_kernel(wavevectors)[:, None]).astype(jnp.bfloat16)

    def finish_group(group):
        table = trig_rows(offsets[group], group, wavevectors)
        longrange = jnp.dot(table, energy, preferred_element_type=jnp.float32) * (8.0 / math.sqrt(WAVES))
        message = jnp.dot(gathered[group].reshape(CELL_LINE * ATOMS, CHANNELS).astype(jnp.bfloat16), w_msg, preferred_element_type=jnp.float32)
        own = masked[group].reshape(CELL_LINE * ATOMS, CHANNELS).astype(jnp.float32)
        result = own + jax.nn.silu(message + longrange)
        result = result * masking[group].reshape(CELL_LINE * ATOMS, 1).astype(jnp.float32)
        return result.astype(jnp.bfloat16).reshape(CELL_LINE, ATOMS, CHANNELS)
    return lax.map(finish_group, groups)
```

```python
import functools
import math

import jax
import jax.numpy as jnp
from jax import lax
from jax.experimental import pallas as pl
from jax.experimental.pallas import tpu as pltpu
from jax.sharding import PartitionSpec as P

MESH = pl.DeviceIdType.MESH
BF = jnp.bfloat16
F32 = jnp.float32

SIN_POLY = (4.442867902973936, -7.30744341898347, 3.594788056349012, -0.7843739717162141)
COS_POLY = (
    1.4142134965673492,
    -6.978850988333631,
    5.739461171609438,
    -1.8835629899115833,
    0.31069819227682083,
)

CHUNK = 256


def cos_sin(turns):
    r = turns - jnp.round(turns)
    u = r * r
    s = SIN_POLY[-1]
    for a in SIN_POLY[-2::-1]:
        s = s * u + a
    s = s * r
    c = COS_POLY[-1]
    for a in COS_POLY[-2::-1]:
        c = c * u + a
    return 1.0 - s * s, s * c


def dot(a, b):
    return jnp.dot(a, b, preferred_element_type=F32)


def kernel(
    dims,
    codes,
    counts,
    feat,
    offs,
    waves,
    radial_hbm,
    w_msg,
    w_mix,
    out,
    win,
    radial,
    table,
    pos,
    aop,
    aop_t,
    wop,
    wop_t,
    kern,
    acc,
    total,
    core_tx,
    core_rx,
    xy_tx,
    xy_rx,
    z_tx,
    z_rx,
    en,
    halo_s,
    halo_r,
    core_s,
    core_r,
    xy_s,
    xy_r,
    z_s,
    z_r,
    ag_s,
    ag_r,
    fw_s,
    fw_r,
    rad_sem,
):
    nx, ny, zh, zl = dims
    nxy, nz = nx * ny, zh * zl
    cells, atoms, chans = feat.shape
    wave_count = waves.shape[1]
    chunks = wave_count // CHUNK
    piece = CHUNK // nxy
    groups, devs = 2 * zl, nx * ny * zh
    line = cells * devs
    wide = cells + 2

    g = lax.axis_index("grp")
    d = lax.axis_index("dev")
    core, my_zl = lax.rem(g, 2), g // 2
    my_x, my_zh, my_y = lax.rem(d, nx), lax.rem(d // nx, zh), d // (nx * zh)
    my_xy = my_y * nx + my_x
    my_z = my_zh * zl + my_zl
    sibling = (g + 1 - 2 * core, d)

    def xy_peer(step):
        j = lax.rem(my_xy + step, nxy)
        return (g, (j // nx) * (nx * zh) + my_zh * nx + lax.rem(j, nx))

    def z_peer(step):
        j = lax.rem(my_z + step, nz)
        return (lax.rem(j, zl) * 2 + core, my_y * (nx * zh) + (j // zl) * nx + my_x)

    steps = [(-1, 0), (1, 0), (0, -1), (0, 1), (-1, -1), (-1, 1), (1, -1), (1, 1)]

    def exists(step):
        a, b = step
        return ((g + a >= 0) & (g + a < groups)) & ((d + b >= 0) & (d + b < devs))

    rad_copy = pltpu.make_async_copy(radial_hbm, radial, rad_sem)
    rad_copy.start()

    barrier = pltpu.get_barrier_semaphore()
    pl.semaphore_signal(barrier, inc=1, device_id=sibling, device_id_type=MESH)

    @pl.loop(1, nxy)
    def _(step):
        pl.semaphore_signal(barrier, inc=1, device_id=xy_peer(step), device_id_type=MESH)

    @pl.loop(1, nz)
    def _(step):
        pl.semaphore_signal(barrier, inc=1, device_id=z_peer(step), device_id_type=MESH)

    greeted = jnp.int32(1 + (nxy - 1) + (nz - 1))
    for step in steps:
        there = exists(step)
        greeted = greeted + there.astype(jnp.int32)

        @pl.when(there)
        def _():
            pl.semaphore_signal(
                barrier, inc=1, device_id=(g + step[0], d + step[1]), device_id_type=MESH
            )

    rows = lax.broadcasted_iota(jnp.int32, (atoms, chans), 0)

    @pl.loop(0, cells)
    def _(i):
        keep = rows < counts[i]
        win[wide + 1 + i] = jnp.where(keep, feat[i].astype(F32), 0.0).astype(BF)

    blank = jnp.zeros((atoms, chans), BF)
    for a, b in steps:

        @pl.when(jnp.logical_not(exists((a, b))))
        def _():
            if b == 0:

                @pl.loop(0, cells)
                def _(i):
                    win[(1 + a) * wide + 1 + i] = blank

            else:
                win[(1 + a) * wide + (0 if b < 0 else wide - 1)] = blank

    pos[...] = jnp.zeros_like(pos)

    @pl.loop(0, cells)
    def _(i):
        o = offs[i]
        at = pl.ds(pl.multiple_of(i * atoms, atoms), atoms)
        x_base = (d * cells + i).astype(F32)
        pos[0:1, at] = (x_base + o[0:1, :]) / line
        pos[1:2, at] = o[1:2, :]
        pos[2:3, at] = (g.astype(F32) + o[2:3, :]) / groups

    high = pos[0:8, :].astype(BF)
    rest = pos[0:8, :] - high.astype(F32)
    middle = rest.astype(BF)
    low = (rest - middle.astype(F32)).astype(BF)
    pos[0:8, :] = high.astype(F32)
    pos[8:16, :] = middle.astype(F32)
    pos[16:24, :] = low.astype(F32)
    aop[...] = pos[...].astype(BF)
    for b in range(cells * atoms // 128):
        aop_t[128 * b : 128 * (b + 1), :] = pos[:, 128 * b : 128 * (b + 1)].T.astype(BF)

    waves_f = waves[...].astype(F32)
    square = jnp.sum(waves_f * waves_f, axis=0, keepdims=True)
    ratio = jnp.exp(-square / 128.0) / (1.0 + square / 64.0)
    wop[...] = jnp.zeros_like(wop)
    for part in range(3):
        wop[8 * part : 8 * part + 3, :] = waves_f
    for b in range(wave_count // 128):
        at = slice(128 * b, 128 * (b + 1))
        wop_t[at, :] = wop[:, at].T.astype(BF)
        kern[at, :] = jnp.broadcast_to(ratio[:, at], (128, 128)).T

    def partial_sums(c):
        acc[c] = jnp.zeros((2, CHUNK, chans), F32)

        @pl.loop(0, cells // 2)
        def _(p):
            at = pl.ds(pl.multiple_of(p * 2 * atoms, 2 * atoms), 2 * atoms)
            mine = win[pl.ds(wide + 1 + 2 * p, 2)].reshape(2 * atoms, chans)
            here = aop[:, at]
            for s in range(0, CHUNK, 64):
                cos, sin = cos_sin(dot(wop_t[c * CHUNK + s : c * CHUNK + s + 64, :], here))
                acc[c, 0, s : s + 64, :] += dot(cos.astype(BF), mine)
                acc[c, 1, s : s + 64, :] += dot(sin.astype(BF), mine)

    def remote(src, dst, send, recv, device):
        return pltpu.make_async_remote_copy(
            src_ref=src, dst_ref=dst, send_sem=send, recv_sem=recv, device_id=device, device_id_type=MESH
        )


    def core_copy(c):
        return remote(core_tx.at[c], core_rx.at[c], core_s.at[c], core_r.at[c], sibling)

    def core_send(c):
        core_tx[c] = acc[c, 1 - core].astype(BF)
        core_copy(c).start()

    def xy_send(c):
        core_copy(c).wait_recv()
        both = acc[c, core] + core_rx[c].astype(F32)
        xy_tx[c] = both.astype(BF)

        @pl.loop(1, nxy)
        def _(step):
            j = lax.rem(my_xy + step, nxy)
            part = pl.ds(pl.multiple_of(j * piece, piece), piece)
            remote(
                xy_tx.at[c, part], xy_rx.at[c, step - 1], xy_s.at[c], xy_r.at[c], xy_peer(step)
            ).start()

    def xy_all(c, send, recv):
        return remote(xy_rx.at[c], xy_rx.at[c], send.at[c], recv.at[c], sibling)

    def z_all(c):
        return remote(z_rx.at[c], z_rx.at[c], z_s.at[c], z_r.at[c], sibling)

    own_part = pl.ds(pl.multiple_of(my_xy * piece, piece), piece)

    def z_send(c):
        xy_all(c, xy_s, xy_r).wait_recv()
        both = xy_tx[c, own_part, :].astype(F32)
        for step in range(nxy - 1):
            both = both + xy_rx[c, step].astype(F32)
        z_tx[c] = both.astype(BF)

        @pl.loop(1, nz)
        def _(step):
            remote(z_tx.at[c], z_rx.at[c, step - 1], z_s.at[c], z_r.at[c], z_peer(step)).start()

    factor_scale = 1.0 / math.sqrt(groups * line * atoms)
    long_scale = 8.0 / math.sqrt(wave_count)

    def ag_send(c):
        z_all(c).wait_recv()
        both = z_tx[c].astype(F32)
        for step in range(nz - 1):
            both = both + z_rx[c, step].astype(F32)
        mixed = dot((both * factor_scale).astype(BF), w_mix[...])
        weight = kern[pl.ds(pl.multiple_of(c * CHUNK + my_xy * piece, piece), piece), :]
        weight = jnp.concatenate([weight] * (chans // 128), axis=1) * long_scale
        en[c, core, own_part, :] = (mixed * weight).astype(BF)

        @pl.loop(1, nxy)
        def _(step):
            mine = en.at[c, core, own_part]
            remote(mine, mine, ag_s.at[c], ag_r.at[c], xy_peer(step)).start()

    def fw_copy(c, which):
        half = en.at[c, which]
        return remote(half, half, fw_s.at[c], fw_r.at[c], sibling)

    def fw_send(c):
        xy_all(c, ag_s, ag_r).wait_recv()
        fw_copy(c, core).start()

    def make_table(c, lo, hi):
        @pl.loop(lo, hi)
        def _(i):
            at = pl.ds(pl.multiple_of(i * atoms, atoms), atoms)
            cols = slice(c * CHUNK, (c + 1) * CHUNK)
            cos, sin = cos_sin(dot(aop_t[at, :], wop[:, cols].astype(BF)))
            table[at, 2 * c * CHUNK : (2 * c + 1) * CHUNK] = cos.astype(BF)
            table[at, (2 * c + 1) * CHUNK : (2 * c + 2) * CHUNK] = sin.astype(BF)

    def short_range(lo, hi):
        pairs = radial.shape[1]

        @pl.loop(lo, hi)
        def _(i):
            gathered = jnp.zeros((atoms, chans), F32)
            for q in range(0, pairs, 2):
                left, right = codes[i * pairs + q], codes[i * pairs + q + 1]
                picked = jnp.concatenate(
                    [win[code // 3 * wide + i + code % 3] for code in (left, right)], axis=0
                )
                blocks = jnp.concatenate([radial[i, q], radial[i, q + 1]], axis=1)
                gathered = gathered + dot(blocks, picked)
            at = pl.ds(pl.multiple_of(i * atoms, atoms), atoms)
            total[at, :] = dot(gathered.astype(BF), w_msg[...])

    def long_range(c):
        fw_copy(c, 1 - core).wait_recv()
        block = 2 * atoms

        @pl.loop(0, cells // 2)
        def _(b):
            at = pl.ds(pl.multiple_of(b * block, block), block)
            rows_taken = table[at, 2 * c * CHUNK : (2 * c + 2) * CHUNK]
            total[at, :] += dot(rows_taken, en[c].reshape(2 * CHUNK, chans))

    def halo_copy(k):
        a, b = steps[k]
        if b == 0:
            src = win.at[pl.ds(wide + 1, cells)]
            dst = win.at[pl.ds((1 - a) * wide + 1, cells)]
        else:
            src = win.at[wide + (cells if b > 0 else 1)]
            dst = win.at[(1 - a) * wide + (0 if b > 0 else wide - 1)]
        return remote(src, dst, halo_s.at[k], halo_r.at[k], (g + a, d + b))

    partial_sums(0)
    pl.semaphore_wait(barrier, greeted)
    core_send(0)
    for k in range(len(steps)):

        @pl.when(exists(steps[k]))
        def _():
            halo_copy(k).start()

    partial_sums(1)
    core_send(1)
    xy_send(0)
    partial_sums(2)
    core_send(2)
    xy_send(1)
    z_send(0)
    partial_sums(3)
    core_send(3)
    xy_send(2)
    z_send(1)
    ag_send(0)
    make_table(0, 0, cells // 2)
    xy_send(3)
    z_send(2)
    ag_send(1)
    make_table(0, cells // 2, cells)
    make_table(1, 0, cells)
    fw_send(0)
    z_send(3)
    ag_send(2)
    make_table(2, 0, cells)
    fw_send(1)

    rad_copy.wait()
    for k in range(len(steps)):
        a, b = steps[k]

        @pl.when(exists((-a, -b)))
        def _():
            halo_copy(k).wait_recv()

    short_range(0, cells // 2)
    ag_send(3)
    short_range(cells // 2, cells)
    fw_send(2)
    make_table(3, 0, cells)
    long_range(0)
    long_range(1)
    fw_send(3)
    long_range(2)
    long_range(3)

    @pl.loop(0, cells)
    def _(i):
        at = pl.ds(pl.multiple_of(i * atoms, atoms), atoms)
        v = total[at, :]
        silu = v / (1.0 + jnp.exp(-v))
        result = win[wide + 1 + i].astype(F32) + silu
        out[i] = jnp.where(rows < counts[i], result, 0.0).astype(BF)

    for k in range(len(steps)):

        @pl.when(exists(steps[k]))
        def _():
            halo_copy(k).wait_send()

    for c in range(chunks):
        core_copy(c).wait_send()
        xy_all(c, xy_s, xy_r).wait_send()
        z_all(c).wait_send()
        xy_all(c, ag_s, ag_r).wait_send()
        fw_copy(c, core).wait_send()


def body(dims, features, offsets, radial, neighbours, counts, wavevectors, w_msg, w_mix):
    nx, ny, zh, zl = dims
    _, cells, atoms, chans = features.shape
    pairs = neighbours.shape[2]
    wave_count = wavevectors.shape[1]
    chunks = wave_count // CHUNK
    nxy, nz = nx * ny, zh * zl
    piece = CHUNK // nxy
    slots = cells * atoms
    smem = pl.BlockSpec(memory_space=pltpu.SMEM)
    vmem = pl.BlockSpec(memory_space=pltpu.VMEM)
    anywhere = pl.BlockSpec(memory_space=pl.ANY)
    dma = pltpu.SemaphoreType.DMA
    updated = pl.pallas_call(
        functools.partial(kernel, dims),
        out_shape=jax.ShapeDtypeStruct((cells, atoms, chans), BF),
        in_specs=[smem, smem, vmem, vmem, vmem, anywhere, vmem, vmem],
        out_specs=vmem,
        scratch_shapes=[
            pltpu.VMEM((3 * (cells + 2), atoms, chans), BF),
            pltpu.VMEM((cells, pairs, atoms, atoms), BF),
            pltpu.VMEM((slots, 2 * wave_count), BF),
            pltpu.VMEM((32, slots), F32),
            pltpu.VMEM((32, slots), BF),
            pltpu.VMEM((slots, 32), BF),
            pltpu.VMEM((32, wave_count), F32),
            pltpu.VMEM((wave_count, 32), BF),
            pltpu.VMEM((wave_count, 128), F32),
            pltpu.VMEM((chunks, 2, CHUNK, chans), F32),
            pltpu.VMEM((slots, chans), F32),
            pltpu.VMEM((chunks, CHUNK, chans), BF),
            pltpu.VMEM((chunks, CHUNK, chans), BF),
            pltpu.VMEM((chunks, CHUNK, chans), BF),
            pltpu.VMEM((chunks, nxy - 1, piece, chans), BF),
            pltpu.VMEM((chunks, piece, chans), BF),
            pltpu.VMEM((chunks, nz - 1, piece, chans), BF),
            pltpu.VMEM((chunks, 2, CHUNK, chans), BF),
            dma((8,)),
            dma((8,)),
        ]
        + [dma((chunks,))] * 10
        + [dma(())],
        compiler_params=pltpu.CompilerParams(
            collective_id=0, has_side_effects=True, vmem_limit_bytes=60000 * 1024
        ),
    )(
        neighbours.reshape(cells * pairs),
        counts.reshape(cells),
        features[0],
        offsets[0],
        wavevectors,
        radial[0],
        w_msg,
        w_mix,
    )
    return updated[None]


def solution(mesh):
    groups, devs = mesh.shape["grp"], mesh.shape["dev"]
    nx = 4 if devs >= 32 else 2
    dims = (nx, devs // (2 * nx), 2, groups // 2)
    in_specs = (
        P("grp", "dev", None, None),
        P("grp", "dev", None, None),
        P("grp", "dev", None, None, None),
        P("grp", "dev", None),
        P("grp", "dev"),
        P(),
        P(),
        P(),
    )
    out_specs = P("grp", "dev", None, None)
    return jax.shard_map(
        functools.partial(body, dims),
        mesh=mesh,
        in_specs=in_specs,
        out_specs=out_specs,
        check_vma=False,
    )
```

```python
import functools
import math

import jax
import jax.numpy as jnp
import numpy as np
from jax import lax
from jax.experimental import pallas as pl
from jax.experimental.pallas import tpu as pltpu
from jax.sharding import PartitionSpec as P

MESH = pl.DeviceIdType.MESH
BF = jnp.bfloat16
F32 = jnp.float32

SIN_POLY = (4.442867902973936, -7.30744341898347, 3.594788056349012, -0.7843739717162141)
COS_POLY = (
    1.4142134965673492,
    -6.978850988333631,
    5.739461171609438,
    -1.8835629899115833,
    0.31069819227682083,
)

CHUNK = 256
REACH = 8
SPAN = 2 * REACH + 1
FINE = 6
BLOCK = 512


def factor_waves():
    entry = np.arange(128)
    waves = np.zeros((32, 2, 128), np.float32)
    for part in range(3):
        waves[8 * part + 0, 0] = np.minimum(entry // FINE, SPAN - 1) - REACH
        waves[8 * part + 1, 0] = entry % FINE
        waves[8 * part + 1, 1] = np.minimum(entry // SPAN, 2) * FINE - REACH
        waves[8 * part + 2, 1] = entry % SPAN - REACH
    return waves.reshape(32, 256)


def cos_sin(turns):
    r = turns - jnp.round(turns)
    u = r * r
    s = SIN_POLY[-1]
    for a in SIN_POLY[-2::-1]:
        s = s * u + a
    s = s * r
    c = COS_POLY[-1]
    for a in COS_POLY[-2::-1]:
        c = c * u + a
    return 1.0 - s * s, s * c


def dot(a, b):
    return jnp.dot(a, b, preferred_element_type=F32)


def kernel(
    dims,
    codes,
    counts,
    feat_hbm,
    offs,
    waves,
    two_waves,
    radial_hbm,
    w_msg,
    w_mix,
    out,
    feat,
    win,
    radial,
    table0,
    table1,
    table2,
    table3,
    pos,
    factors,
    one_hot,
    kern,
    acc,
    total,
    core_tx,
    core_rx,
    xy_tx,
    xy_rx,
    z_tx,
    z_rx,
    en,
    halo_s,
    halo_r,
    core_s,
    core_r,
    xy_s,
    xy_r,
    z_s,
    z_r,
    ag_s,
    ag_r,
    fw_s,
    fw_r,
    feat_sem,
    rad_sem,
):
    nx, ny, zh, zl = dims
    nxy, nz = nx * ny, zh * zl
    cells, atoms, chans = feat.shape
    wave_count = waves.shape[1]
    chunks = wave_count // CHUNK
    piece = CHUNK // nxy
    groups, devs = 2 * zl, nx * ny * zh
    line = cells * devs
    wide = cells + 2

    g = lax.axis_index("grp")
    d = lax.axis_index("dev")
    core, my_zl = lax.rem(g, 2), g // 2
    my_x, my_zh, my_y = lax.rem(d, nx), lax.rem(d // nx, zh), d // (nx * zh)
    my_xy = my_y * nx + my_x
    my_z = my_zh * zl + my_zl
    sibling = (g + 1 - 2 * core, d)

    def xy_peer(step):
        j = lax.rem(my_xy + step, nxy)
        return (g, (j // nx) * (nx * zh) + my_zh * nx + lax.rem(j, nx))

    def z_peer(step):
        j = lax.rem(my_z + step, nz)
        return (lax.rem(j, zl) * 2 + core, my_y * (nx * zh) + (j // zl) * nx + my_x)

    steps = [(-1, 0), (1, 0), (0, -1), (0, 1), (-1, -1), (-1, 1), (1, -1), (1, 1)]

    def exists(step):
        a, b = step
        return ((g + a >= 0) & (g + a < groups)) & ((d + b >= 0) & (d + b < devs))

    tables = (table0, table1, table2, table3)
    feat_copy = pltpu.make_async_copy(feat_hbm, feat, feat_sem)
    feat_copy.start()
    rad_copy = pltpu.make_async_copy(radial_hbm, radial, rad_sem)
    rad_copy.start()

    barrier = pltpu.get_barrier_semaphore()
    pl.semaphore_signal(barrier, inc=1, device_id=sibling, device_id_type=MESH)

    @pl.loop(1, nxy)
    def _(step):
        pl.semaphore_signal(barrier, inc=1, device_id=xy_peer(step), device_id_type=MESH)

    @pl.loop(1, nz)
    def _(step):
        pl.semaphore_signal(barrier, inc=1, device_id=z_peer(step), device_id_type=MESH)

    greeted = jnp.int32(1 + (nxy - 1) + (nz - 1))
    for step in steps:
        there = exists(step)
        greeted = greeted + there.astype(jnp.int32)

        @pl.when(there)
        def _():
            pl.semaphore_signal(
                barrier, inc=1, device_id=(g + step[0], d + step[1]), device_id_type=MESH
            )

    pos[...] = jnp.zeros_like(pos)
    cell_ids = lax.broadcasted_iota(jnp.int32, (cells, atoms), 0)
    planes = (
        ((d * cells + cell_ids).astype(F32) + offs[0]) / line,
        offs[1],
        (g.astype(F32) + offs[2]) / groups,
    )
    for axis, plane in enumerate(planes):
        for part in range(3):
            rounded = plane.astype(BF).astype(F32)
            plane = plane - rounded
            for i in range(cells):
                pos[8 * part + axis : 8 * part + axis + 1, atoms * i : atoms * (i + 1)] = rounded[
                    i : i + 1
                ]

    ky = waves[1:2, :] + REACH
    coarse = (ky >= FINE).astype(jnp.int32) + (ky >= 2 * FINE).astype(jnp.int32)
    places = (
        (waves[0:1, :] + REACH) * FINE + ky - FINE * coarse,
        coarse * SPAN + waves[2:3, :] + REACH,
    )
    for which, place in enumerate(places):
        for lo in range(0, wave_count, CHUNK):
            entry = lax.broadcasted_iota(jnp.int32, (128, CHUNK), 0)
            hot = jnp.where(entry == place[:, lo : lo + CHUNK], 1.0, 0.0).astype(BF)
            one_hot[which, 0:128, lo : lo + CHUNK] = hot
            one_hot[which, 128:256, lo : lo + CHUNK] = hot

    waves_f = waves[...].astype(F32)
    square = jnp.sum(waves_f * waves_f, axis=0, keepdims=True)
    ratio = jnp.exp(-square / 128.0) / (1.0 + square / 64.0)
    for b in range(wave_count // 128):
        at = slice(128 * b, 128 * (b + 1))
        kern[at, :] = jnp.broadcast_to(ratio[:, at], (128, 128)).T

    block = min(BLOCK, cells * atoms)
    blocks = cells * atoms // block

    def rows_of(b):
        return pl.ds(pl.multiple_of(b * block, block), block)

    def first_dims(a, b):
        return lax.dot_general(a, b, (((0,), (0,)), ((), ())), preferred_element_type=F32)

    @pl.loop(0, blocks)
    def _(b):
        turns = first_dims(pos[:, rows_of(b)].astype(BF), two_waves[...])
        for which in range(2):
            for k, value in enumerate(cos_sin(turns[:, 128 * which : 128 * (which + 1)])):
                high = value.astype(BF)
                factors[which, k, rows_of(b), 0:128] = high
                factors[which, k, rows_of(b), 128:256] = (value - high.astype(F32)).astype(BF)

    rows = lax.broadcasted_iota(jnp.int32, (atoms, chans), 0)
    feat_copy.wait()

    @pl.loop(0, cells)
    def _(i):
        keep = rows < counts[i]
        win[wide + 1 + i] = jnp.where(keep, feat[i].astype(F32), 0.0).astype(BF)

    blank = jnp.zeros((atoms, chans), BF)
    for a, b in steps:

        @pl.when(jnp.logical_not(exists((a, b))))
        def _():
            if b == 0:

                @pl.loop(0, cells)
                def _(i):
                    win[(1 + a) * wide + 1 + i] = blank

            else:
                win[(1 + a) * wide + (0 if b < 0 else wide - 1)] = blank

    def make_table(c):
        cols = slice(c * CHUNK, (c + 1) * CHUNK)

        @pl.loop(0, blocks)
        def _(b):
            at = rows_of(b)
            (c1, s1), (c2, s2) = (
                [dot(factors[which, k, at, :], one_hot[which, :, cols]) for k in range(2)]
                for which in range(2)
            )
            tables[c][at, 0:CHUNK] = (c1 * c2 - s1 * s2).astype(BF)
            tables[c][at, CHUNK : 2 * CHUNK] = (c1 * s2 + s1 * c2).astype(BF)

    def partial_sums(c):
        mine = win[wide + 1 : wide + 1 + cells].reshape(cells * atoms, chans)
        acc[c] = first_dims(tables[c][...], mine).reshape(2, CHUNK, chans)

    def remote(src, dst, send, recv, device):
        return pltpu.make_async_remote_copy(
            src_ref=src, dst_ref=dst, send_sem=send, recv_sem=recv, device_id=device, device_id_type=MESH
        )


    def core_copy(c):
        return remote(core_tx.at[c], core_rx.at[c], core_s.at[c], core_r.at[c], sibling)

    def core_send(c):
        core_tx[c] = acc[c, 1 - core].astype(BF)
        core_copy(c).start()

    def xy_send(c):
        core_copy(c).wait_recv()
        both = acc[c, core] + core_rx[c].astype(F32)
        xy_tx[c] = both.astype(BF)

        @pl.loop(1, nxy)
        def _(step):
            j = lax.rem(my_xy + step, nxy)
            part = pl.ds(pl.multiple_of(j * piece, piece), piece)
            remote(
                xy_tx.at[c, part], xy_rx.at[c, step - 1], xy_s.at[c], xy_r.at[c], xy_peer(step)
            ).start()

    def xy_all(c, send, recv):
        return remote(xy_rx.at[c], xy_rx.at[c], send.at[c], recv.at[c], sibling)

    def z_all(c):
        return remote(z_rx.at[c], z_rx.at[c], z_s.at[c], z_r.at[c], sibling)

    own_part = pl.ds(pl.multiple_of(my_xy * piece, piece), piece)

    def z_send(c):
        xy_all(c, xy_s, xy_r).wait_recv()
        both = xy_tx[c, own_part, :].astype(F32)
        for step in range(nxy - 1):
            both = both + xy_rx[c, step].astype(F32)
        z_tx[c] = both.astype(BF)

        @pl.loop(1, nz)
        def _(step):
            remote(z_tx.at[c], z_rx.at[c, step - 1], z_s.at[c], z_r.at[c], z_peer(step)).start()

    factor_scale = 1.0 / math.sqrt(groups * line * atoms)
    long_scale = 8.0 / math.sqrt(wave_count)

    def ag_send(c):
        z_all(c).wait_recv()
        both = z_tx[c].astype(F32)
        for step in range(nz - 1):
            both = both + z_rx[c, step].astype(F32)
        mixed = dot((both * factor_scale).astype(BF), w_mix[...])
        weight = kern[pl.ds(pl.multiple_of(c * CHUNK + my_xy * piece, piece), piece), :]
        weight = jnp.concatenate([weight] * (chans // 128), axis=1) * long_scale
        en[c, core, own_part, :] = (mixed * weight).astype(BF)

        @pl.loop(1, nxy)
        def _(step):
            mine = en.at[c, core, own_part]
            remote(mine, mine, ag_s.at[c], ag_r.at[c], xy_peer(step)).start()

    def fw_copy(c, which):
        half = en.at[c, which]
        return remote(half, half, fw_s.at[c], fw_r.at[c], sibling)

    def fw_send(c):
        xy_all(c, ag_s, ag_r).wait_recv()
        fw_copy(c, core).start()

    def short_range(lo, hi):
        pairs = radial.shape[1]

        @pl.loop(lo, hi, step=2)
        def _(first):
            for i in (first, first + 1):
                gathered = jnp.zeros((atoms, chans), F32)
                for q in range(0, pairs, 2):
                    left, right = codes[q, i], codes[q + 1, i]
                    picked = jnp.concatenate(
                        [win[code // 3 * wide + i + code % 3] for code in (left, right)], axis=0
                    )
                    matrix = jnp.concatenate([radial[i, q], radial[i, q + 1]], axis=1)
                    gathered = gathered + dot(matrix, picked)
                at = pl.ds(pl.multiple_of(i * atoms, atoms), atoms)
                total[at, :] = dot(gathered.astype(BF), w_msg[...])

    def long_range(c):
        fw_copy(c, 1 - core).wait_recv()

        @pl.loop(0, blocks)
        def _(b):
            total[rows_of(b), :] += dot(tables[c][rows_of(b), :], en[c].reshape(2 * CHUNK, chans))

    def halo_copy(k):
        a, b = steps[k]
        if b == 0:
            src = win.at[pl.ds(wide + 1, cells)]
            dst = win.at[pl.ds((1 - a) * wide + 1, cells)]
        else:
            src = win.at[wide + (cells if b > 0 else 1)]
            dst = win.at[(1 - a) * wide + (0 if b > 0 else wide - 1)]
        return remote(src, dst, halo_s.at[k], halo_r.at[k], (g + a, d + b))

    make_table(0)
    partial_sums(0)
    pl.semaphore_wait(barrier, greeted)
    core_send(0)
    for k in range(len(steps)):

        @pl.when(exists(steps[k]))
        def _():
            halo_copy(k).start()

    make_table(1)
    partial_sums(1)
    core_send(1)
    xy_send(0)
    make_table(2)
    partial_sums(2)
    core_send(2)
    xy_send(1)
    make_table(3)
    partial_sums(3)
    core_send(3)
    z_send(0)
    xy_send(2)
    xy_send(3)
    z_send(1)
    ag_send(0)
    z_send(2)
    ag_send(1)
    z_send(3)
    fw_send(0)
    ag_send(2)
    fw_send(1)

    rad_copy.wait()
    for k in range(len(steps)):
        a, b = steps[k]

        @pl.when(exists((-a, -b)))
        def _():
            halo_copy(k).wait_recv()

    short_range(0, cells)
    ag_send(3)
    fw_send(2)
    long_range(0)
    long_range(1)
    long_range(2)
    fw_send(3)
    long_range(3)

    @pl.loop(0, cells)
    def _(i):
        at = pl.ds(pl.multiple_of(i * atoms, atoms), atoms)
        v = total[at, :]
        silu = v / (1.0 + jnp.exp(-v))
        out[i] = (win[wide + 1 + i].astype(F32) + silu).astype(BF)

    for k in range(len(steps)):

        @pl.when(exists(steps[k]))
        def _():
            halo_copy(k).wait_send()

    for c in range(chunks):
        core_copy(c).wait_send()
        xy_all(c, xy_s, xy_r).wait_send()
        z_all(c).wait_send()
        xy_all(c, ag_s, ag_r).wait_send()
        fw_copy(c, core).wait_send()


def body(dims, features, offsets, radial, neighbours, counts, wavevectors, w_msg, w_mix):
    nx, ny, zh, zl = dims
    _, cells, atoms, chans = features.shape
    pairs = neighbours.shape[2]
    wave_count = wavevectors.shape[1]
    chunks = wave_count // CHUNK
    nxy, nz = nx * ny, zh * zl
    piece = CHUNK // nxy
    slots = cells * atoms
    smem = pl.BlockSpec(memory_space=pltpu.SMEM)
    vmem = pl.BlockSpec(memory_space=pltpu.VMEM)
    anywhere = pl.BlockSpec(memory_space=pl.ANY)
    dma = pltpu.SemaphoreType.DMA
    updated = pl.pallas_call(
        functools.partial(kernel, dims),
        out_shape=jax.ShapeDtypeStruct((cells, atoms, chans), BF),
        in_specs=[smem, smem, anywhere, vmem, vmem, vmem, anywhere, vmem, vmem],
        out_specs=vmem,
        scratch_shapes=[
            pltpu.VMEM((cells, atoms, chans), BF),
            pltpu.VMEM((3 * (cells + 2), atoms, chans), BF),
            pltpu.VMEM((cells, pairs, atoms, atoms), BF),
        ]
        + [pltpu.VMEM((slots, 2 * CHUNK), BF)] * chunks
        + [
            pltpu.VMEM((32, slots), F32),
            pltpu.VMEM((2, 2, slots, 256), BF),
            pltpu.VMEM((2, 256, wave_count), BF),
            pltpu.VMEM((wave_count, 128), F32),
            pltpu.VMEM((chunks, 2, CHUNK, chans), F32),
            pltpu.VMEM((slots, chans), F32),
            pltpu.VMEM((chunks, CHUNK, chans), BF),
            pltpu.VMEM((chunks, CHUNK, chans), BF),
            pltpu.VMEM((chunks, CHUNK, chans), BF),
            pltpu.VMEM((chunks, nxy - 1, piece, chans), BF),
            pltpu.VMEM((chunks, piece, chans), BF),
            pltpu.VMEM((chunks, nz - 1, piece, chans), BF),
            pltpu.VMEM((chunks, 2, CHUNK, chans), BF),
            dma((8,)),
            dma((8,)),
        ]
        + [dma((chunks,))] * 10
        + [dma(())] * 2,
        compiler_params=pltpu.CompilerParams(
            collective_id=0, has_side_effects=True, vmem_limit_bytes=60000 * 1024
        ),
    )(
        neighbours[0].T,
        counts.reshape(cells),
        features[0],
        jnp.transpose(offsets[0], (1, 0, 2)),
        wavevectors,
        jnp.asarray(factor_waves(), BF),
        radial[0],
        w_msg,
        w_mix,
    )
    slot_ids = jnp.arange(atoms, dtype=jnp.int32)
    present = slot_ids[None, :, None] < counts.reshape(cells, 1, 1)
    return jnp.where(present, updated, jnp.zeros_like(updated))[None]


def solution(mesh):
    groups, devs = mesh.shape["grp"], mesh.shape["dev"]
    nx = 4 if devs >= 32 else 2
    dims = (nx, devs // (2 * nx), 2, groups // 2)
    in_specs = (
        P("grp", "dev", None, None),
        P("grp", "dev", None, None),
        P("grp", "dev", None, None, None),
        P("grp", "dev", None),
        P("grp", "dev"),
        P(),
        P(),
        P(),
    )
    out_specs = P("grp", "dev", None, None)
    return jax.shard_map(
        functools.partial(body, dims),
        mesh=mesh,
        in_specs=in_specs,
        out_specs=out_specs,
        check_vma=False,
    )
```

```python
import functools
import math

import jax
import jax.numpy as jnp
from jax import lax
from jax.experimental import pallas as pl
from jax.experimental.pallas import tpu as pltpu
from jax.sharding import PartitionSpec as P

MESH = pl.DeviceIdType.MESH
BF = jnp.bfloat16
F32 = jnp.float32

SIN_POLY = (4.442867902973936, -7.30744341898347, 3.594788056349012, -0.7843739717162141)
COS_POLY = (
    1.4142134965673492,
    -6.978850988333631,
    5.739461171609438,
    -1.8835629899115833,
    0.31069819227682083,
)

CHUNK = 256
BLOCK = 1024


def cos_sin(turns):
    r = turns - jnp.round(turns)
    u = r * r
    s = SIN_POLY[-1]
    for a in SIN_POLY[-2::-1]:
        s = s * u + a
    s = s * r
    c = COS_POLY[-1]
    for a in COS_POLY[-2::-1]:
        c = c * u + a
    return 1.0 - s * s, s * c


def dot(a, b):
    return jnp.dot(a, b, preferred_element_type=F32)


def kernel(
    dims,
    codes,
    counts,
    feat_hbm,
    offs,
    waves,
    radial_hbm,
    w_msg,
    w_mix,
    out,
    feat,
    win,
    radial,
    table0,
    table1,
    table2,
    table3,
    pos,
    wop,
    kern,
    acc,
    total,
    core_tx,
    core_rx,
    xy_tx,
    xy_rx,
    z_tx,
    z_rx,
    en,
    halo_s,
    halo_r,
    core_s,
    core_r,
    xy_s,
    xy_r,
    z_s,
    z_r,
    ag_s,
    ag_r,
    fw_s,
    fw_r,
    feat_sem,
    rad_sem,
):
    nx, ny, zh, zl = dims
    nxy, nz = nx * ny, zh * zl
    cells, atoms, chans = feat.shape
    wave_count = waves.shape[1]
    chunks = wave_count // CHUNK
    piece = CHUNK // nxy
    groups, devs = 2 * zl, nx * ny * zh
    line = cells * devs
    wide = cells + 2

    g = lax.axis_index("grp")
    d = lax.axis_index("dev")
    core, my_zl = lax.rem(g, 2), g // 2
    my_x, my_zh, my_y = lax.rem(d, nx), lax.rem(d // nx, zh), d // (nx * zh)
    my_xy = my_y * nx + my_x
    my_z = my_zh * zl + my_zl
    sibling = (g + 1 - 2 * core, d)

    def xy_peer(step):
        j = lax.rem(my_xy + step, nxy)
        return (g, (j // nx) * (nx * zh) + my_zh * nx + lax.rem(j, nx))

    def z_peer(step):
        j = lax.rem(my_z + step, nz)
        return (lax.rem(j, zl) * 2 + core, my_y * (nx * zh) + (j // zl) * nx + my_x)

    steps = [(-1, 0), (1, 0), (0, -1), (0, 1)]

    def exists(step):
        a, b = step
        return ((g + a >= 0) & (g + a < groups)) & ((d + b >= 0) & (d + b < devs))

    tables = (table0, table1, table2, table3)
    feat_copy = pltpu.make_async_copy(feat_hbm, feat, feat_sem)
    feat_copy.start()
    rad_copy = pltpu.make_async_copy(radial_hbm, radial, rad_sem)
    rad_copy.start()

    barrier = pltpu.get_barrier_semaphore()
    pl.semaphore_signal(barrier, inc=1, device_id=sibling, device_id_type=MESH)

    @pl.loop(1, nxy)
    def _(step):
        pl.semaphore_signal(barrier, inc=1, device_id=xy_peer(step), device_id_type=MESH)

    @pl.loop(1, nz)
    def _(step):
        pl.semaphore_signal(barrier, inc=1, device_id=z_peer(step), device_id_type=MESH)

    greeted = jnp.int32(1 + (nxy - 1) + (nz - 1))
    for step in steps:
        there = exists(step)
        greeted = greeted + there.astype(jnp.int32)

        @pl.when(there)
        def _():
            pl.semaphore_signal(
                barrier, inc=1, device_id=(g + step[0], d + step[1]), device_id_type=MESH
            )

    rows = lax.broadcasted_iota(jnp.int32, (atoms, chans), 0)
    feat_copy.wait()

    @pl.loop(0, cells)
    def _(i):
        keep = rows < counts[i]
        win[wide + 1 + i] = jnp.where(keep, feat[i].astype(F32), 0.0).astype(BF)

    blank = jnp.zeros((atoms, chans), BF)
    for a in (-1, 1):

        @pl.when(jnp.logical_not(exists((a, 0))))
        def _():
            @pl.loop(0, wide)
            def _(i):
                win[(1 + a) * wide + i] = blank

    for b, end in ((-1, 0), (1, wide - 1)):

        @pl.when(jnp.logical_not(exists((0, b))))
        def _():
            win[wide + end] = blank

    def remote(src, dst, send, recv, device):
        return pltpu.make_async_remote_copy(
            src_ref=src, dst_ref=dst, send_sem=send, recv_sem=recv, device_id=device, device_id_type=MESH
        )


    def core_copy(c):
        return remote(core_tx.at[c], core_rx.at[c], core_s.at[c], core_r.at[c], sibling)

    def core_send(c):
        core_tx[c] = acc[c, 1 - core].astype(BF)
        core_copy(c).start()

    def xy_send(c):
        core_copy(c).wait_recv()
        both = acc[c, core] + core_rx[c].astype(F32)
        xy_tx[c] = both.astype(BF)

        @pl.loop(1, nxy)
        def _(step):
            j = lax.rem(my_xy + step, nxy)
            part = pl.ds(pl.multiple_of(j * piece, piece), piece)
            remote(
                xy_tx.at[c, part], xy_rx.at[c, step - 1], xy_s.at[c], xy_r.at[c], xy_peer(step)
            ).start()

    def xy_all(c, send, recv):
        return remote(xy_rx.at[c], xy_rx.at[c], send.at[c], recv.at[c], sibling)

    def z_all(c):
        return remote(z_rx.at[c], z_rx.at[c], z_s.at[c], z_r.at[c], sibling)

    own_part = pl.ds(pl.multiple_of(my_xy * piece, piece), piece)

    def z_send(c):
        xy_all(c, xy_s, xy_r).wait_recv()
        both = xy_tx[c, own_part, :].astype(F32)
        for step in range(nxy - 1):
            both = both + xy_rx[c, step].astype(F32)
        z_tx[c] = both.astype(BF)

        @pl.loop(1, nz)
        def _(step):
            remote(z_tx.at[c], z_rx.at[c, step - 1], z_s.at[c], z_r.at[c], z_peer(step)).start()

    factor_scale = 1.0 / math.sqrt(groups * line * atoms)
    long_scale = 8.0 / math.sqrt(wave_count)

    def ag_send(c):
        z_all(c).wait_recv()
        both = z_tx[c].astype(F32)
        for step in range(nz - 1):
            both = both + z_rx[c, step].astype(F32)
        mixed = dot((both * factor_scale).astype(BF), w_mix[...])
        weight = kern[pl.ds(pl.multiple_of(c * CHUNK + my_xy * piece, piece), piece), :]
        weight = jnp.concatenate([weight] * (chans // 128), axis=1) * long_scale
        en[c, core, own_part, :] = (mixed * weight).astype(BF)

        @pl.loop(1, nxy)
        def _(step):
            mine = en.at[c, core, own_part]
            remote(mine, mine, ag_s.at[c], ag_r.at[c], xy_peer(step)).start()

    def fw_copy(c, which):
        half = en.at[c, which]
        return remote(half, half, fw_s.at[c], fw_r.at[c], sibling)

    def fw_send(c):
        xy_all(c, ag_s, ag_r).wait_recv()
        fw_copy(c, core).start()

    def short_cell(i):
        pairs = radial.shape[1]
        gathered = jnp.zeros((atoms, chans), F32)
        for q in range(0, pairs, 2):
            left, right = codes[q, i], codes[q + 1, i]
            picked = jnp.concatenate(
                [win[code // 3 * wide + i + code % 3] for code in (left, right)], axis=0
            )
            matrix = jnp.concatenate([radial[i, q], radial[i, q + 1]], axis=1)
            gathered = gathered + dot(matrix, picked)
        at = pl.ds(pl.multiple_of(i * atoms, atoms), atoms)
        total[at, :] = dot(gathered.astype(BF), w_msg[...])

    def short_range(lo, hi):
        @pl.loop(lo, hi, step=2)
        def _(first):
            short_cell(first)
            short_cell(first + 1)

    def long_range(c):
        fw_copy(c, 1 - core).wait_recv()

        @pl.loop(0, blocks)
        def _(b):
            total[rows_of(b), :] += dot(tables[c][rows_of(b), :], en[c].reshape(2 * CHUNK, chans))

    def finish(c):
        fw_copy(c, 1 - core).wait_recv()

        @pl.loop(0, blocks)
        def _(b):
            v = total[rows_of(b), :]
            v = v + dot(tables[c][rows_of(b), :], en[c].reshape(2 * CHUNK, chans))
            silu = v / (1.0 + jnp.exp(-v))
            first = b * (block // atoms)
            own = win[pl.ds(wide + 1 + first, block // atoms)].reshape(block, chans).astype(F32)
            out[pl.ds(first, block // atoms)] = (
                (own + silu).astype(BF).reshape(block // atoms, atoms, chans)
            )

    def halo_copy(k):
        a, b = steps[k]
        if b == 0:
            src = win.at[pl.ds(wide + 1, cells)]
            dst = win.at[pl.ds((1 - a) * wide + 1, cells)]
        else:
            src = win.at[wide + (cells if b > 0 else 1)]
            dst = win.at[wide + (0 if b > 0 else wide - 1)]
        return remote(src, dst, halo_s.at[k], halo_r.at[k], (g + a, d + b))

    def relay_copy(k, end):
        a, _ = steps[k]
        at = wide - 1 if end else 0
        which = 4 + 2 * k + end
        return remote(
            win.at[wide + at],
            win.at[(1 - a) * wide + at],
            halo_s.at[which],
            halo_r.at[which],
            (g + a, d),
        )

    def both_relays(k, act):
        for end in range(2):
            act(relay_copy(k, end))

    def relay_edges():
        for k in (2, 3):

            @pl.when(exists(steps[5 - k]))
            def _():
                halo_copy(k).wait_recv()

        for k in (0, 1):

            @pl.when(exists(steps[k]))
            def _():
                both_relays(k, lambda copy: copy.start())

    def slabs_arrived():
        for k in (0, 1):

            @pl.when(exists(steps[1 - k]))
            def _():
                halo_copy(k).wait_recv()

    def relays_arrived():
        for k in (0, 1):

            @pl.when(exists(steps[1 - k]))
            def _():
                both_relays(k, lambda copy: copy.wait_recv())

    pl.semaphore_wait(barrier, greeted)
    for k in (2, 3, 0, 1):

        @pl.when(exists(steps[k]))
        def _():
            halo_copy(k).start()

    pos[...] = jnp.zeros_like(pos)
    cell_ids = lax.broadcasted_iota(jnp.int32, (cells, atoms), 0)
    planes = (
        ((d * cells + cell_ids).astype(F32) + offs[0]) / line,
        offs[1],
        (g.astype(F32) + offs[2]) / groups,
    )
    for axis, plane in enumerate(planes):
        for part in range(3):
            rounded = plane.astype(BF).astype(F32)
            plane = plane - rounded
            for i in range(cells):
                pos[8 * part + axis : 8 * part + axis + 1, atoms * i : atoms * (i + 1)] = rounded[
                    i : i + 1
                ]
    waves_f = waves[...].astype(F32)
    wop[...] = jnp.zeros_like(wop)
    for part in range(3):
        wop[8 * part : 8 * part + 3, :] = waves_f

    def first_dims(a, b):
        return lax.dot_general(a, b, (((0,), (0,)), ((), ())), preferred_element_type=F32)

    slots = cells * atoms
    block = min(BLOCK, slots)
    blocks = slots // block

    def rows_of(b):
        return pl.ds(pl.multiple_of(b * block, block), block)

    def make_table(c, step=256):
        turning = wop[:, c * CHUNK : (c + 1) * CHUNK].astype(BF)
        for lo in range(0, slots, step):
            cos, sin = cos_sin(first_dims(pos[:, lo : lo + step].astype(BF), turning))
            tables[c][lo : lo + step, 0:CHUNK] = cos.astype(BF)
            tables[c][lo : lo + step, CHUNK : 2 * CHUNK] = sin.astype(BF)

    def damping():
        square = jnp.sum(waves_f * waves_f, axis=0, keepdims=True)
        ratio = jnp.exp(-square / 128.0) / (1.0 + square / 64.0)
        for b in range(wave_count // 128):
            at = slice(128 * b, 128 * (b + 1))
            kern[at, :] = jnp.broadcast_to(ratio[:, at], (128, 128)).T

    def partial_sums(c):
        mine = win[wide + 1 : wide + 1 + cells].reshape(cells * atoms, chans)
        acc[c] = first_dims(tables[c][...], mine).reshape(2, CHUNK, chans)

    make_table(0)
    make_table(1)
    partial_sums(0)
    core_send(0)
    relay_edges()
    make_table(2)
    partial_sums(1)
    core_send(1)
    xy_send(0)
    make_table(3)
    partial_sums(2)
    core_send(2)
    xy_send(1)
    partial_sums(3)
    core_send(3)
    xy_send(2)
    damping()
    xy_send(3)
    z_send(0)
    z_send(1)
    z_send(2)
    ag_send(0)
    rad_copy.wait()
    slabs_arrived()
    relays_arrived()
    short_range(0, cells // 4)
    z_send(3)
    ag_send(1)
    short_range(cells // 4, cells // 2)
    ag_send(2)
    fw_send(0)
    short_range(cells // 2, 3 * cells // 4)
    ag_send(3)
    fw_send(1)
    short_range(3 * cells // 4, cells)
    long_range(0)
    fw_send(2)
    long_range(1)
    fw_send(3)
    long_range(2)
    finish(3)

    for k in range(len(steps)):

        @pl.when(exists(steps[k]))
        def _():
            halo_copy(k).wait_send()
            if k < 2:
                both_relays(k, lambda copy: copy.wait_send())

    for c in range(chunks):
        core_copy(c).wait_send()
        xy_all(c, xy_s, xy_r).wait_send()
        z_all(c).wait_send()
        xy_all(c, ag_s, ag_r).wait_send()
        fw_copy(c, core).wait_send()


def body(dims, features, offsets, radial, neighbours, counts, wavevectors, w_msg, w_mix):
    nx, ny, zh, zl = dims
    _, cells, atoms, chans = features.shape
    pairs = neighbours.shape[2]
    wave_count = wavevectors.shape[1]
    chunks = wave_count // CHUNK
    nxy, nz = nx * ny, zh * zl
    piece = CHUNK // nxy
    slots = cells * atoms
    smem = pl.BlockSpec(memory_space=pltpu.SMEM)
    vmem = pl.BlockSpec(memory_space=pltpu.VMEM)
    anywhere = pl.BlockSpec(memory_space=pl.ANY)
    dma = pltpu.SemaphoreType.DMA
    updated = pl.pallas_call(
        functools.partial(kernel, dims),
        out_shape=jax.ShapeDtypeStruct((cells, atoms, chans), BF),
        in_specs=[smem, smem, anywhere, vmem, vmem, anywhere, vmem, vmem],
        out_specs=vmem,
        scratch_shapes=[
            pltpu.VMEM((cells, atoms, chans), BF),
            pltpu.VMEM((3 * (cells + 2), atoms, chans), BF),
            pltpu.VMEM((cells, pairs, atoms, atoms), BF),
        ]
        + [pltpu.VMEM((slots, 2 * CHUNK), BF)] * chunks
        + [
            pltpu.VMEM((32, slots), F32),
            pltpu.VMEM((32, wave_count), F32),
            pltpu.VMEM((wave_count, 128), F32),
            pltpu.VMEM((chunks, 2, CHUNK, chans), F32),
            pltpu.VMEM((slots, chans), F32),
            pltpu.VMEM((chunks, CHUNK, chans), BF),
            pltpu.VMEM((chunks, CHUNK, chans), BF),
            pltpu.VMEM((chunks, CHUNK, chans), BF),
            pltpu.VMEM((chunks, nxy - 1, piece, chans), BF),
            pltpu.VMEM((chunks, piece, chans), BF),
            pltpu.VMEM((chunks, nz - 1, piece, chans), BF),
            pltpu.VMEM((chunks, 2, CHUNK, chans), BF),
            dma((8,)),
            dma((8,)),
        ]
        + [dma((chunks,))] * 10
        + [dma(())] * 2,
        compiler_params=pltpu.CompilerParams(
            collective_id=0, has_side_effects=True, vmem_limit_bytes=60000 * 1024
        ),
    )(
        neighbours[0].T,
        counts.reshape(cells),
        features[0],
        jnp.transpose(offsets[0], (1, 0, 2)),
        wavevectors,
        radial[0],
        w_msg,
        w_mix,
    )
    slot_ids = jnp.arange(atoms, dtype=jnp.int32)
    present = slot_ids[None, :, None] < counts.reshape(cells, 1, 1)
    return jnp.where(present, updated, jnp.zeros_like(updated))[None]


def solution(mesh):
    groups, devs = mesh.shape["grp"], mesh.shape["dev"]
    nx = 4 if devs >= 32 else 2
    dims = (nx, devs // (2 * nx), 2, groups // 2)
    in_specs = (
        P("grp", "dev", None, None),
        P("grp", "dev", None, None),
        P("grp", "dev", None, None, None),
        P("grp", "dev", None),
        P("grp", "dev"),
        P(),
        P(),
        P(),
    )
    out_specs = P("grp", "dev", None, None)
    return jax.shard_map(
        functools.partial(body, dims),
        mesh=mesh,
        in_specs=in_specs,
        out_specs=out_specs,
        check_vma=False,
    )
```

```python
import functools
import math

import jax
import jax.numpy as jnp
from jax import lax
from jax.experimental import pallas as pl
from jax.experimental.pallas import tpu as pltpu
from jax.sharding import PartitionSpec as P

MESH = pl.DeviceIdType.MESH
BF = jnp.bfloat16
F32 = jnp.float32

SIN_POLY = (4.442867902973936, -7.30744341898347, 3.594788056349012, -0.7843739717162141)
COS_POLY = (
    1.4142134965673492,
    -6.978850988333631,
    5.739461171609438,
    -1.8835629899115833,
    0.31069819227682083,
)

CHUNK = 256
BLOCK = 1024


def cos_sin(turns):
    r = turns - jnp.round(turns)
    u = r * r
    s = SIN_POLY[-1]
    for a in SIN_POLY[-2::-1]:
        s = s * u + a
    s = s * r
    c = COS_POLY[-1]
    for a in COS_POLY[-2::-1]:
        c = c * u + a
    return 1.0 - s * s, s * c


def dot(a, b):
    return jnp.dot(a, b, preferred_element_type=F32)


def kernel(
    dims,
    codes,
    counts,
    feat_hbm,
    offs,
    waves,
    radial_hbm,
    w_msg,
    w_mix,
    out,
    feat,
    win,
    radial,
    table0,
    table1,
    table2,
    table3,
    pos,
    wop,
    kern,
    acc,
    total,
    core_tx,
    core_rx,
    xy_tx,
    xy_rx,
    z_tx,
    z_rx,
    en,
    halo_s,
    halo_r,
    core_s,
    core_r,
    xy_s,
    xy_r,
    z_s,
    z_r,
    ag_s,
    ag_r,
    fw_s,
    fw_r,
    feat_sem,
    rad_sem,
):
    nx, ny, zh, zl = dims
    nxy, nz = nx * ny, zh * zl
    cells, atoms, chans = feat.shape
    wave_count = waves.shape[1]
    chunks = wave_count // CHUNK
    piece = CHUNK // nxy
    groups, devs = 2 * zl, nx * ny * zh
    line = cells * devs
    wide = cells + 2

    g = lax.axis_index("grp")
    d = lax.axis_index("dev")
    core, my_zl = lax.rem(g, 2), g // 2
    my_x, my_zh, my_y = lax.rem(d, nx), lax.rem(d // nx, zh), d // (nx * zh)
    my_xy = my_y * nx + my_x
    my_z = my_zh * zl + my_zl
    sibling = (g + 1 - 2 * core, d)

    def xy_peer(step):
        j = lax.rem(my_xy + step, nxy)
        return (g, (j // nx) * (nx * zh) + my_zh * nx + lax.rem(j, nx))

    def z_peer(step):
        j = lax.rem(my_z + step, nz)
        return (lax.rem(j, zl) * 2 + core, my_y * (nx * zh) + (j // zl) * nx + my_x)

    steps = [(-1, 0), (1, 0), (0, -1), (0, 1)]

    def exists(step):
        a, b = step
        return ((g + a >= 0) & (g + a < groups)) & ((d + b >= 0) & (d + b < devs))

    tables = (table0, table1, table2, table3)
    feat_copy = pltpu.make_async_copy(feat_hbm, feat, feat_sem)
    feat_copy.start()
    rad_copy = pltpu.make_async_copy(radial_hbm, radial, rad_sem)
    rad_copy.start()

    barrier = pltpu.get_barrier_semaphore()
    pl.semaphore_signal(barrier, inc=1, device_id=sibling, device_id_type=MESH)

    @pl.loop(1, nxy)
    def _(step):
        pl.semaphore_signal(barrier, inc=1, device_id=xy_peer(step), device_id_type=MESH)

    @pl.loop(1, nz)
    def _(step):
        pl.semaphore_signal(barrier, inc=1, device_id=z_peer(step), device_id_type=MESH)

    greeted = jnp.int32(1 + (nxy - 1) + (nz - 1))
    for step in steps:
        there = exists(step)
        greeted = greeted + there.astype(jnp.int32)

        @pl.when(there)
        def _():
            pl.semaphore_signal(
                barrier, inc=1, device_id=(g + step[0], d + step[1]), device_id_type=MESH
            )

    def remote(src, dst, send, recv, device):
        return pltpu.make_async_remote_copy(
            src_ref=src, dst_ref=dst, send_sem=send, recv_sem=recv, device_id=device, device_id_type=MESH
        )


    def core_copy(c):
        return remote(core_tx.at[c], core_rx.at[c], core_s.at[c], core_r.at[c], sibling)

    def core_send(c):
        core_tx[c] = acc[c, 1 - core].astype(BF)
        core_copy(c).start()

    def xy_send(c):
        core_copy(c).wait_recv()
        both = acc[c, core] + core_rx[c].astype(F32)
        xy_tx[c] = both.astype(BF)

        @pl.loop(1, nxy)
        def _(step):
            j = lax.rem(my_xy + step, nxy)
            part = pl.ds(pl.multiple_of(j * piece, piece), piece)
            remote(
                xy_tx.at[c, part], xy_rx.at[c, step - 1], xy_s.at[c], xy_r.at[c], xy_peer(step)
            ).start()

    def xy_all(c, send, recv):
        return remote(xy_rx.at[c], xy_rx.at[c], send.at[c], recv.at[c], sibling)

    def z_all(c):
        return remote(z_rx.at[c], z_rx.at[c], z_s.at[c], z_r.at[c], sibling)

    own_part = pl.ds(pl.multiple_of(my_xy * piece, piece), piece)

    def z_send(c):
        xy_all(c, xy_s, xy_r).wait_recv()
        both = xy_tx[c, own_part, :].astype(F32)
        for step in range(nxy - 1):
            both = both + xy_rx[c, step].astype(F32)
        z_tx[c] = both.astype(BF)

        @pl.loop(1, nz)
        def _(step):
            remote(z_tx.at[c], z_rx.at[c, step - 1], z_s.at[c], z_r.at[c], z_peer(step)).start()

    factor_scale = 1.0 / math.sqrt(groups * line * atoms)
    long_scale = 8.0 / math.sqrt(wave_count)

    def ag_send(c):
        z_all(c).wait_recv()
        both = z_tx[c].astype(F32)
        for step in range(nz - 1):
            both = both + z_rx[c, step].astype(F32)
        mixed = dot((both * factor_scale).astype(BF), w_mix[...])
        weight = kern[pl.ds(pl.multiple_of(c * CHUNK + my_xy * piece, piece), piece), :]
        weight = jnp.concatenate([weight] * (chans // 128), axis=1) * long_scale
        en[c, core, own_part, :] = (mixed * weight).astype(BF)

        @pl.loop(1, nxy)
        def _(step):
            mine = en.at[c, core, own_part]
            remote(mine, mine, ag_s.at[c], ag_r.at[c], xy_peer(step)).start()

    def fw_copy(c, which):
        half = en.at[c, which]
        return remote(half, half, fw_s.at[c], fw_r.at[c], sibling)

    def fw_send(c):
        xy_all(c, ag_s, ag_r).wait_recv()
        fw_copy(c, core).start()

    def short_cell(i):
        pairs = radial.shape[1]
        gathered = jnp.zeros((atoms, chans), F32)
        for q in range(0, pairs, 2):
            left, right = codes[q, i], codes[q + 1, i]
            picked = jnp.concatenate(
                [win[code // 3 * wide + i + code % 3] for code in (left, right)], axis=0
            )
            matrix = jnp.concatenate([radial[i, q], radial[i, q + 1]], axis=1)
            gathered = gathered + dot(matrix, picked)
        at = pl.ds(pl.multiple_of(i * atoms, atoms), atoms)
        total[at, :] = dot(gathered.astype(BF), w_msg[...])

    def short_range(lo, hi):
        @pl.loop(lo, hi, step=2)
        def _(first):
            short_cell(first)
            short_cell(first + 1)

    def long_range(c):
        fw_copy(c, 1 - core).wait_recv()

        @pl.loop(0, blocks)
        def _(b):
            total[rows_of(b), :] += dot(tables[c][rows_of(b), :], en[c].reshape(2 * CHUNK, chans))

    def finish(c):
        fw_copy(c, 1 - core).wait_recv()

        @pl.loop(0, blocks)
        def _(b):
            v = total[rows_of(b), :]
            v = v + dot(tables[c][rows_of(b), :], en[c].reshape(2 * CHUNK, chans))
            silu = v / (1.0 + jnp.exp(-v))
            first = b * (block // atoms)
            own = win[pl.ds(wide + 1 + first, block // atoms)].reshape(block, chans).astype(F32)
            result = (own + silu).reshape(block // atoms, atoms, chans)
            for i in range(block // atoms):
                out[first + i] = jnp.where(rows < counts[first + i], result[i], 0.0).astype(BF)

    def halo_copy(k):
        _, b = steps[k]
        src = win.at[wide + (cells if b > 0 else 1)]
        dst = win.at[wide + (0 if b > 0 else wide - 1)]
        return remote(src, dst, halo_s.at[k], halo_r.at[k], (g, d + b))

    early = 7 * cells // 8

    def slab_copy(k, part):
        a, _ = steps[k]
        lo, count = (early, cells - early) if part else (0, early)
        which = k + 8 * part
        return remote(
            win.at[pl.ds(wide + 1 + lo, count)],
            win.at[pl.ds((1 - a) * wide + 1 + lo, count)],
            halo_s.at[which],
            halo_r.at[which],
            (g + a, d),
        )

    def start_halo():
        for k in (2, 3):

            @pl.when(exists(steps[k]))
            def _():
                halo_copy(k).start()

        for k in (0, 1):

            @pl.when(exists(steps[k]))
            def _():
                slab_copy(k, 0).start()

            @pl.when(exists(steps[k]) & (core != k))
            def _():
                slab_copy(k, 1).start()

    def start_rest():
        for k in (0, 1):

            @pl.when(exists(steps[k]) & (core == k))
            def _():
                slab_copy(k, 1).start()

    def relay_copy(k, end):
        a, _ = steps[k]
        at = wide - 1 if end else 0
        which = 4 + 2 * k + end
        return remote(
            win.at[wide + at],
            win.at[(1 - a) * wide + at],
            halo_s.at[which],
            halo_r.at[which],
            (g + a, d),
        )

    def both_relays(k, act):
        for end in range(2):
            act(relay_copy(k, end))

    def relay_edges():
        for k in (2, 3):

            @pl.when(exists(steps[5 - k]))
            def _():
                halo_copy(k).wait_recv()

        for k in (0, 1):

            @pl.when(exists(steps[k]))
            def _():
                both_relays(k, lambda copy: copy.start())

    def slabs_arrived():
        for k in (0, 1):

            @pl.when(exists(steps[1 - k]))
            def _():
                slab_copy(k, 0).wait_recv()
                slab_copy(k, 1).wait_recv()

    def relays_arrived():
        for k in (0, 1):

            @pl.when(exists(steps[1 - k]))
            def _():
                both_relays(k, lambda copy: copy.wait_recv())

    pos[...] = jnp.zeros_like(pos)
    cell_ids = lax.broadcasted_iota(jnp.int32, (cells, atoms), 0)
    planes = (
        ((d * cells + cell_ids).astype(F32) + offs[0]) / line,
        offs[1],
        (g.astype(F32) + offs[2]) / groups,
    )
    for axis, plane in enumerate(planes):
        for part in range(3):
            rounded = plane.astype(BF).astype(F32)
            plane = plane - rounded
            for i in range(cells):
                pos[8 * part + axis : 8 * part + axis + 1, atoms * i : atoms * (i + 1)] = rounded[
                    i : i + 1
                ]
    waves_f = waves[...].astype(F32)
    wop[...] = jnp.zeros_like(wop)
    for part in range(3):
        wop[8 * part : 8 * part + 3, :] = waves_f

    def first_dims(a, b):
        return lax.dot_general(a, b, (((0,), (0,)), ((), ())), preferred_element_type=F32)

    slots = cells * atoms
    block = min(BLOCK, slots)
    blocks = slots // block

    def rows_of(b):
        return pl.ds(pl.multiple_of(b * block, block), block)

    def make_table(c, step=256):
        turning = wop[:, c * CHUNK : (c + 1) * CHUNK].astype(BF)
        for lo in range(0, slots, step):
            cos, sin = cos_sin(first_dims(pos[:, lo : lo + step].astype(BF), turning))
            tables[c][lo : lo + step, 0:CHUNK] = cos.astype(BF)
            tables[c][lo : lo + step, CHUNK : 2 * CHUNK] = sin.astype(BF)

    def damping():
        square = jnp.sum(waves_f * waves_f, axis=0, keepdims=True)
        ratio = jnp.exp(-square / 128.0) / (1.0 + square / 64.0)
        for b in range(wave_count // 128):
            at = slice(128 * b, 128 * (b + 1))
            kern[at, :] = jnp.broadcast_to(ratio[:, at], (128, 128)).T

    def partial_sums(c):
        mine = win[wide + 1 : wide + 1 + cells].reshape(cells * atoms, chans)
        acc[c] = first_dims(tables[c][...], mine).reshape(2, CHUNK, chans)

    make_table(0)

    rows = lax.broadcasted_iota(jnp.int32, (atoms, chans), 0)
    feat_copy.wait()

    @pl.loop(0, cells)
    def _(i):
        keep = rows < counts[i]
        win[wide + 1 + i] = jnp.where(keep, feat[i].astype(F32), 0.0).astype(BF)

    blank = jnp.zeros((atoms, chans), BF)
    for a in (-1, 1):

        @pl.when(jnp.logical_not(exists((a, 0))))
        def _():
            @pl.loop(0, wide)
            def _(i):
                win[(1 + a) * wide + i] = blank

    for b, end in ((-1, 0), (1, wide - 1)):

        @pl.when(jnp.logical_not(exists((0, b))))
        def _():
            win[wide + end] = blank

    pl.semaphore_wait(barrier, greeted)
    start_halo()
    make_table(1)
    partial_sums(0)
    core_send(0)
    make_table(2)
    partial_sums(1)
    core_send(1)
    xy_send(0)
    make_table(3)
    partial_sums(2)
    core_send(2)
    xy_send(1)
    partial_sums(3)
    core_send(3)
    xy_send(2)
    damping()
    xy_send(3)
    z_send(0)
    z_send(1)
    z_send(2)
    z_send(3)
    relay_edges()
    start_rest()
    rad_copy.wait()
    ag_send(0)
    ag_send(1)
    ag_send(2)
    ag_send(3)
    fw_send(0)
    fw_send(1)
    slabs_arrived()
    relays_arrived()
    short_range(0, cells // 2)
    fw_send(2)
    short_range(cells // 2, cells)
    fw_send(3)
    long_range(0)
    long_range(1)
    long_range(2)
    finish(3)

    for k in (0, 1):

        @pl.when(exists(steps[k]))
        def _():
            slab_copy(k, 0).wait_send()
            slab_copy(k, 1).wait_send()
            both_relays(k, lambda copy: copy.wait_send())

    for k in (2, 3):

        @pl.when(exists(steps[k]))
        def _():
            halo_copy(k).wait_send()

    for c in range(chunks):
        core_copy(c).wait_send()
        xy_all(c, xy_s, xy_r).wait_send()
        z_all(c).wait_send()
        xy_all(c, ag_s, ag_r).wait_send()
        fw_copy(c, core).wait_send()


def body(dims, features, offsets, radial, neighbours, counts, wavevectors, w_msg, w_mix):
    nx, ny, zh, zl = dims
    _, cells, atoms, chans = features.shape
    pairs = neighbours.shape[2]
    wave_count = wavevectors.shape[1]
    chunks = wave_count // CHUNK
    nxy, nz = nx * ny, zh * zl
    piece = CHUNK // nxy
    slots = cells * atoms
    smem = pl.BlockSpec(memory_space=pltpu.SMEM)
    vmem = pl.BlockSpec(memory_space=pltpu.VMEM)
    anywhere = pl.BlockSpec(memory_space=pl.ANY)
    dma = pltpu.SemaphoreType.DMA
    updated = pl.pallas_call(
        functools.partial(kernel, dims),
        out_shape=jax.ShapeDtypeStruct((cells, atoms, chans), BF),
        in_specs=[smem, smem, anywhere, vmem, vmem, anywhere, vmem, vmem],
        out_specs=vmem,
        scratch_shapes=[
            pltpu.VMEM((cells, atoms, chans), BF),
            pltpu.VMEM((3 * (cells + 2), atoms, chans), BF),
            pltpu.VMEM((cells, pairs, atoms, atoms), BF),
        ]
        + [pltpu.VMEM((slots, 2 * CHUNK), BF)] * chunks
        + [
            pltpu.VMEM((32, slots), F32),
            pltpu.VMEM((32, wave_count), F32),
            pltpu.VMEM((wave_count, 128), F32),
            pltpu.VMEM((chunks, 2, CHUNK, chans), F32),
            pltpu.VMEM((slots, chans), F32),
            pltpu.VMEM((chunks, CHUNK, chans), BF),
            pltpu.VMEM((chunks, CHUNK, chans), BF),
            pltpu.VMEM((chunks, CHUNK, chans), BF),
            pltpu.VMEM((chunks, nxy - 1, piece, chans), BF),
            pltpu.VMEM((chunks, piece, chans), BF),
            pltpu.VMEM((chunks, nz - 1, piece, chans), BF),
            pltpu.VMEM((chunks, 2, CHUNK, chans), BF),
            dma((10,)),
            dma((10,)),
        ]
        + [dma((chunks,))] * 10
        + [dma(())] * 2,
        compiler_params=pltpu.CompilerParams(
            collective_id=0, has_side_effects=True, vmem_limit_bytes=60000 * 1024
        ),
    )(
        neighbours[0].T,
        counts.reshape(cells),
        features[0],
        jnp.transpose(offsets[0], (1, 0, 2)),
        wavevectors,
        radial[0],
        w_msg,
        w_mix,
    )
    return updated[None]


def solution(mesh):
    groups, devs = mesh.shape["grp"], mesh.shape["dev"]
    nx = 4 if devs >= 32 else 2
    dims = (nx, devs // (2 * nx), 2, groups // 2)
    in_specs = (
        P("grp", "dev", None, None),
        P("grp", "dev", None, None),
        P("grp", "dev", None, None, None),
        P("grp", "dev", None),
        P("grp", "dev"),
        P(),
        P(),
        P(),
    )
    out_specs = P("grp", "dev", None, None)
    return jax.shard_map(
        functools.partial(body, dims),
        mesh=mesh,
        in_specs=in_specs,
        out_specs=out_specs,
        check_vma=False,
    )
```

```python
import functools
import math

import jax
import jax.numpy as jnp
from jax import lax
from jax.experimental import pallas as pl
from jax.experimental.pallas import tpu as pltpu
from jax.sharding import PartitionSpec as P

MESH = pl.DeviceIdType.MESH
BF = jnp.bfloat16
F32 = jnp.float32

SIN_POLY = (4.442867902973936, -7.30744341898347, 3.594788056349012, -0.7843739717162141)
COS_POLY = (
    1.4142134965673492,
    -6.978850988333631,
    5.739461171609438,
    -1.8835629899115833,
    0.31069819227682083,
)

CHUNK = 256
BLOCK = 1024


def cos_sin(turns):
    r = turns - jnp.round(turns)
    u = r * r
    s = SIN_POLY[-1]
    for a in SIN_POLY[-2::-1]:
        s = s * u + a
    s = s * r
    c = COS_POLY[-1]
    for a in COS_POLY[-2::-1]:
        c = c * u + a
    return 1.0 - s * s, s * c


def dot(a, b):
    return jnp.dot(a, b, preferred_element_type=F32)


def kernel(
    dims,
    codes,
    counts,
    feat_hbm,
    offs,
    waves,
    radial_hbm,
    w_msg,
    w_mix,
    out,
    feat,
    win,
    radial,
    table0,
    table1,
    table2,
    table3,
    pos,
    wop,
    kern,
    acc,
    total,
    core_tx,
    core_rx,
    xy_tx,
    xy_rx,
    z_tx,
    z_rx,
    en,
    halo_s,
    halo_r,
    core_s,
    core_r,
    xy_s,
    xy_r,
    z_s,
    z_r,
    ag_s,
    ag_r,
    fw_s,
    fw_r,
    feat_sem,
    rad_sem,
    out_sem,
):
    nx, ny, zh, zl = dims
    nxy, nz = nx * ny, zh * zl
    cells, atoms, chans = feat.shape
    wave_count = waves.shape[1]
    chunks = wave_count // CHUNK
    piece = CHUNK // nxy
    groups, devs = 2 * zl, nx * ny * zh
    line = cells * devs
    wide = cells + 2

    g = lax.axis_index("grp")
    d = lax.axis_index("dev")
    core, my_zl = lax.rem(g, 2), g // 2
    my_x, my_zh, my_y = lax.rem(d, nx), lax.rem(d // nx, zh), d // (nx * zh)
    my_xy = my_y * nx + my_x
    my_z = my_zh * zl + my_zl
    sibling = (g + 1 - 2 * core, d)

    def xy_peer(step):
        j = lax.rem(my_xy + step, nxy)
        return (g, (j // nx) * (nx * zh) + my_zh * nx + lax.rem(j, nx))

    def z_peer(step):
        j = lax.rem(my_z + step, nz)
        return (lax.rem(j, zl) * 2 + core, my_y * (nx * zh) + (j // zl) * nx + my_x)

    steps = [(-1, 0), (1, 0), (0, -1), (0, 1)]

    def exists(step):
        a, b = step
        return ((g + a >= 0) & (g + a < groups)) & ((d + b >= 0) & (d + b < devs))

    tables = (table0, table1, table2, table3)
    feat_copy = pltpu.make_async_copy(feat_hbm, feat, feat_sem)
    feat_copy.start()
    rad_copy = pltpu.make_async_copy(radial_hbm, radial, rad_sem)
    rad_copy.start()

    barrier = pltpu.get_barrier_semaphore()
    greeted = jnp.int32(1 + (nxy - 1) + (nz - 1))
    for step in steps:
        there = exists(step)
        greeted = greeted + there.astype(jnp.int32)

        @pl.when(there)
        def _():
            pl.semaphore_signal(
                barrier, inc=1, device_id=(g + step[0], d + step[1]), device_id_type=MESH
            )

    def remote(src, dst, send, recv, device):
        return pltpu.make_async_remote_copy(
            src_ref=src, dst_ref=dst, send_sem=send, recv_sem=recv, device_id=device, device_id_type=MESH
        )


    def core_copy(c):
        return remote(core_tx.at[c], core_rx.at[c], core_s.at[c], core_r.at[c], sibling)

    def core_send(c):
        core_tx[c] = acc[c, 1 - core].astype(BF)
        core_copy(c).start()

    def xy_send(c):
        core_copy(c).wait_recv()
        both = acc[c, core] + core_rx[c].astype(F32)
        xy_tx[c] = both.astype(BF)

        @pl.loop(1, nxy)
        def _(step):
            j = lax.rem(my_xy + step, nxy)
            part = pl.ds(pl.multiple_of(j * piece, piece), piece)
            remote(
                xy_tx.at[c, part], xy_rx.at[c, step - 1], xy_s.at[c], xy_r.at[c], xy_peer(step)
            ).start()

    def xy_all(c, send, recv):
        return remote(xy_rx.at[c], xy_rx.at[c], send.at[c], recv.at[c], sibling)

    def z_all(c):
        return remote(z_rx.at[c], z_rx.at[c], z_s.at[c], z_r.at[c], sibling)

    own_part = pl.ds(pl.multiple_of(my_xy * piece, piece), piece)

    def z_send(c):
        xy_all(c, xy_s, xy_r).wait_recv()
        both = xy_tx[c, own_part, :].astype(F32)
        for step in range(nxy - 1):
            both = both + xy_rx[c, step].astype(F32)
        z_tx[c] = both.astype(BF)

        @pl.loop(1, nz)
        def _(step):
            remote(z_tx.at[c], z_rx.at[c, step - 1], z_s.at[c], z_r.at[c], z_peer(step)).start()

    factor_scale = 1.0 / math.sqrt(groups * line * atoms)
    long_scale = 8.0 / math.sqrt(wave_count)

    def ag_send(c):
        z_all(c).wait_recv()
        both = z_tx[c].astype(F32)
        for step in range(nz - 1):
            both = both + z_rx[c, step].astype(F32)
        mixed = dot((both * factor_scale).astype(BF), w_mix[...])
        weight = kern[pl.ds(pl.multiple_of(c * CHUNK + my_xy * piece, piece), piece), :]
        weight = jnp.concatenate([weight] * (chans // 128), axis=1) * long_scale
        en[c, core, own_part, :] = (mixed * weight).astype(BF)

        @pl.loop(1, nxy)
        def _(step):
            mine = en.at[c, core, own_part]
            remote(mine, mine, ag_s.at[c], ag_r.at[c], xy_peer(step)).start()

    def fw_copy(c, which):
        half = en.at[c, which]
        return remote(half, half, fw_s.at[c], fw_r.at[c], sibling)

    def fw_send(c):
        xy_all(c, ag_s, ag_r).wait_recv()
        fw_copy(c, core).start()

    def short_cell(i):
        pairs = radial.shape[1]
        gathered = jnp.zeros((atoms, chans), F32)
        for q in range(0, pairs, 2):
            left, right = codes[q, i], codes[q + 1, i]
            picked = jnp.concatenate(
                [win[code // 3 * wide + i + code % 3] for code in (left, right)], axis=0
            )
            matrix = jnp.concatenate([radial[i, q], radial[i, q + 1]], axis=1)
            gathered = gathered + dot(matrix, picked)
        at = pl.ds(pl.multiple_of(i * atoms, atoms), atoms)
        total[at, :] = dot(gathered.astype(BF), w_msg[...])

    def short_range(lo, hi):
        @pl.loop(lo, hi, step=2)
        def _(first):
            short_cell(first)
            short_cell(first + 1)

    def long_range(c):
        fw_copy(c, 1 - core).wait_recv()

        @pl.loop(0, blocks)
        def _(b):
            total[rows_of(b), :] += dot(tables[c][rows_of(b), :], en[c].reshape(2 * CHUNK, chans))

    def out_copy(b):
        at = pl.ds(b * (block // atoms), block // atoms)
        return pltpu.make_async_copy(feat.at[at], out.at[at], out_sem.at[b])

    def finish(c):
        fw_copy(c, 1 - core).wait_recv()

        @pl.loop(0, blocks)
        def _(b):
            v = total[rows_of(b), :]
            v = v + dot(tables[c][rows_of(b), :], en[c].reshape(2 * CHUNK, chans))
            silu = v / (1.0 + jnp.exp(-v))
            first = b * (block // atoms)
            own = win[pl.ds(wide + 1 + first, block // atoms)].reshape(block, chans).astype(F32)
            result = (own + silu).reshape(block // atoms, atoms, chans)
            for i in range(block // atoms):
                feat[first + i] = jnp.where(rows < counts[first + i], result[i], 0.0).astype(BF)
            out_copy(b).start()

        for b in range(blocks):
            out_copy(b).wait()

    def halo_copy(k):
        _, b = steps[k]
        src = win.at[wide + (cells if b > 0 else 1)]
        dst = win.at[wide + (0 if b > 0 else wide - 1)]
        return remote(src, dst, halo_s.at[k], halo_r.at[k], (g, d + b))

    early = 7 * cells // 8

    def slab_copy(k, part):
        a, _ = steps[k]
        lo, count = (early, cells - early) if part else (0, early)
        which = k + 8 * part
        return remote(
            win.at[pl.ds(wide + 1 + lo, count)],
            win.at[pl.ds((1 - a) * wide + 1 + lo, count)],
            halo_s.at[which],
            halo_r.at[which],
            (g + a, d),
        )

    def start_halo():
        for k in (2, 3):

            @pl.when(exists(steps[k]))
            def _():
                halo_copy(k).start()

        for k in (0, 1):

            @pl.when(exists(steps[k]))
            def _():
                slab_copy(k, 0).start()

            @pl.when(exists(steps[k]) & (core != k))
            def _():
                slab_copy(k, 1).start()

    def start_rest():
        for k in (0, 1):

            @pl.when(exists(steps[k]) & (core == k))
            def _():
                slab_copy(k, 1).start()

    def relay_copy(k, end):
        a, _ = steps[k]
        at = wide - 1 if end else 0
        which = 4 + 2 * k + end
        return remote(
            win.at[wide + at],
            win.at[(1 - a) * wide + at],
            halo_s.at[which],
            halo_r.at[which],
            (g + a, d),
        )

    def both_relays(k, act):
        for end in range(2):
            act(relay_copy(k, end))

    def relay_edges():
        for k in (2, 3):

            @pl.when(exists(steps[5 - k]))
            def _():
                halo_copy(k).wait_recv()

        for k in (0, 1):

            @pl.when(exists(steps[k]))
            def _():
                both_relays(k, lambda copy: copy.start())

    def slabs_arrived():
        for k in (0, 1):

            @pl.when(exists(steps[1 - k]))
            def _():
                slab_copy(k, 0).wait_recv()
                slab_copy(k, 1).wait_recv()

    def relays_arrived():
        for k in (0, 1):

            @pl.when(exists(steps[1 - k]))
            def _():
                both_relays(k, lambda copy: copy.wait_recv())

    @pl.loop(1, nz)
    def _(step):
        pl.semaphore_signal(barrier, inc=1, device_id=z_peer(step), device_id_type=MESH)

    @pl.loop(1, nxy)
    def _(step):
        pl.semaphore_signal(barrier, inc=1, device_id=xy_peer(step), device_id_type=MESH)

    pl.semaphore_signal(barrier, inc=1, device_id=sibling, device_id_type=MESH)

    pos[...] = jnp.zeros_like(pos)
    cell_ids = lax.broadcasted_iota(jnp.int32, (cells, atoms), 0)
    planes = (
        ((d * cells + cell_ids).astype(F32) + offs[0]) / line,
        offs[1],
        (g.astype(F32) + offs[2]) / groups,
    )
    for axis, plane in enumerate(planes):
        for part in range(3):
            rounded = plane.astype(BF).astype(F32)
            plane = plane - rounded
            for i in range(cells):
                pos[8 * part + axis : 8 * part + axis + 1, atoms * i : atoms * (i + 1)] = rounded[
                    i : i + 1
                ]
    waves_f = waves[...].astype(F32)
    wop[...] = jnp.zeros_like(wop)
    for part in range(3):
        wop[8 * part : 8 * part + 3, :] = waves_f

    def first_dims(a, b):
        return lax.dot_general(a, b, (((0,), (0,)), ((), ())), preferred_element_type=F32)

    slots = cells * atoms
    block = min(BLOCK, slots)
    blocks = slots // block

    def rows_of(b):
        return pl.ds(pl.multiple_of(b * block, block), block)

    def make_table(c, step=256):
        turning = wop[:, c * CHUNK : (c + 1) * CHUNK].astype(BF)
        for lo in range(0, slots, step):
            cos, sin = cos_sin(first_dims(pos[:, lo : lo + step].astype(BF), turning))
            tables[c][lo : lo + step, 0:CHUNK] = cos.astype(BF)
            tables[c][lo : lo + step, CHUNK : 2 * CHUNK] = sin.astype(BF)

    def damping():
        square = jnp.sum(waves_f * waves_f, axis=0, keepdims=True)
        ratio = jnp.exp(-square / 128.0) / (1.0 + square / 64.0)
        for b in range(wave_count // 128):
            at = slice(128 * b, 128 * (b + 1))
            kern[at, :] = jnp.broadcast_to(ratio[:, at], (128, 128)).T

    def partial_sums(c):
        mine = win[wide + 1 : wide + 1 + cells].reshape(cells * atoms, chans)
        acc[c] = first_dims(tables[c][...], mine).reshape(2, CHUNK, chans)

    make_table(0)

    rows = lax.broadcasted_iota(jnp.int32, (atoms, chans), 0)
    feat_copy.wait()

    @pl.loop(0, cells)
    def _(i):
        keep = rows < counts[i]
        win[wide + 1 + i] = jnp.where(keep, feat[i].astype(F32), 0.0).astype(BF)

    blank = jnp.zeros((atoms, chans), BF)
    for a in (-1, 1):

        @pl.when(jnp.logical_not(exists((a, 0))))
        def _():
            @pl.loop(0, wide)
            def _(i):
                win[(1 + a) * wide + i] = blank

    for b, end in ((-1, 0), (1, wide - 1)):

        @pl.when(jnp.logical_not(exists((0, b))))
        def _():
            win[wide + end] = blank

    pl.semaphore_wait(barrier, greeted)
    start_halo()
    make_table(1)
    partial_sums(0)
    core_send(0)
    make_table(2)
    partial_sums(1)
    core_send(1)
    xy_send(0)
    make_table(3)
    partial_sums(2)
    core_send(2)
    xy_send(1)
    partial_sums(3)
    core_send(3)
    xy_send(2)
    xy_send(3)
    damping()
    z_send(0)
    z_send(1)
    z_send(2)
    relay_edges()
    z_send(3)
    start_rest()
    rad_copy.wait()
    ag_send(0)
    ag_send(1)
    ag_send(2)
    ag_send(3)
    fw_send(0)
    fw_send(1)
    slabs_arrived()
    relays_arrived()
    short_range(0, cells // 2)
    fw_send(2)
    short_range(cells // 2, 3 * cells // 4)
    fw_send(3)
    short_range(3 * cells // 4, cells)
    long_range(0)
    long_range(1)
    long_range(2)
    finish(3)

    for k in (0, 1):

        @pl.when(exists(steps[k]))
        def _():
            slab_copy(k, 0).wait_send()
            slab_copy(k, 1).wait_send()
            both_relays(k, lambda copy: copy.wait_send())

    for k in (2, 3):

        @pl.when(exists(steps[k]))
        def _():
            halo_copy(k).wait_send()

    for c in range(chunks):
        core_copy(c).wait_send()
        xy_all(c, xy_s, xy_r).wait_send()
        z_all(c).wait_send()
        xy_all(c, ag_s, ag_r).wait_send()
        fw_copy(c, core).wait_send()


def copy_kernel(parts, source, result, held, in_sem, out_sem):
    coming = [pltpu.make_async_copy(source.at[p], held.at[p], in_sem.at[p]) for p in parts]
    going = [pltpu.make_async_copy(held.at[p], result.at[p], out_sem.at[p]) for p in parts]
    for copy in coming:
        copy.start()
    for first, second in zip(coming, going):
        first.wait()
        second.start()
    for copy in going:
        copy.wait()


def copied(array, parts=4):
    split = array.reshape(parts, -1, *array.shape[1:])
    anywhere = pl.BlockSpec(memory_space=pl.ANY)
    return pl.pallas_call(
        functools.partial(copy_kernel, range(parts)),
        out_shape=jax.ShapeDtypeStruct(split.shape, split.dtype),
        in_specs=[anywhere],
        out_specs=anywhere,
        scratch_shapes=[
            pltpu.VMEM(split.shape, split.dtype),
            pltpu.SemaphoreType.DMA((parts,)),
            pltpu.SemaphoreType.DMA((parts,)),
        ],
        compiler_params=pltpu.CompilerParams(vmem_limit_bytes=60000 * 1024),
    )(split).reshape(array.shape)


def body(dims, features, offsets, radial, neighbours, counts, wavevectors, w_msg, w_mix):
    nx, ny, zh, zl = dims
    _, cells, atoms, chans = features.shape
    pairs = neighbours.shape[2]
    wave_count = wavevectors.shape[1]
    chunks = wave_count // CHUNK
    nxy, nz = nx * ny, zh * zl
    piece = CHUNK // nxy
    slots = cells * atoms
    smem = pl.BlockSpec(memory_space=pltpu.SMEM)
    vmem = pl.BlockSpec(memory_space=pltpu.VMEM)
    anywhere = pl.BlockSpec(memory_space=pl.ANY)
    dma = pltpu.SemaphoreType.DMA
    updated = pl.pallas_call(
        functools.partial(kernel, dims),
        out_shape=jax.ShapeDtypeStruct((cells, atoms, chans), BF),
        in_specs=[smem, smem, anywhere, vmem, vmem, anywhere, vmem, vmem],
        out_specs=anywhere,
        scratch_shapes=[
            pltpu.VMEM((cells, atoms, chans), BF),
            pltpu.VMEM((3 * (cells + 2), atoms, chans), BF),
            pltpu.VMEM((cells, pairs, atoms, atoms), BF),
        ]
        + [pltpu.VMEM((slots, 2 * CHUNK), BF)] * chunks
        + [
            pltpu.VMEM((32, slots), F32),
            pltpu.VMEM((32, wave_count), F32),
            pltpu.VMEM((wave_count, 128), F32),
            pltpu.VMEM((chunks, 2, CHUNK, chans), F32),
            pltpu.VMEM((slots, chans), F32),
            pltpu.VMEM((chunks, CHUNK, chans), BF),
            pltpu.VMEM((chunks, CHUNK, chans), BF),
            pltpu.VMEM((chunks, CHUNK, chans), BF),
            pltpu.VMEM((chunks, nxy - 1, piece, chans), BF),
            pltpu.VMEM((chunks, piece, chans), BF),
            pltpu.VMEM((chunks, nz - 1, piece, chans), BF),
            pltpu.VMEM((chunks, 2, CHUNK, chans), BF),
            dma((10,)),
            dma((10,)),
        ]
        + [dma((chunks,))] * 10
        + [dma(())] * 2
        + [dma((max(1, slots // BLOCK),))],
        compiler_params=pltpu.CompilerParams(
            collective_id=0, has_side_effects=True, vmem_limit_bytes=60000 * 1024
        ),
    )(
        neighbours[0].T,
        counts.reshape(cells),
        features[0],
        jnp.transpose(offsets[0], (1, 0, 2)),
        wavevectors,
        radial[0],
        w_msg,
        w_mix,
    )
    return copied(updated)[None]


def solution(mesh):
    groups, devs = mesh.shape["grp"], mesh.shape["dev"]
    nx = 4 if devs >= 32 else 2
    dims = (nx, devs // (2 * nx), 2, groups // 2)
    in_specs = (
        P("grp", "dev", None, None),
        P("grp", "dev", None, None),
        P("grp", "dev", None, None, None),
        P("grp", "dev", None),
        P("grp", "dev"),
        P(),
        P(),
        P(),
    )
    out_specs = P("grp", "dev", None, None)
    return jax.shard_map(
        functools.partial(body, dims),
        mesh=mesh,
        in_specs=in_specs,
        out_specs=out_specs,
        check_vma=False,
    )
```

```python
import functools
import math

import jax
import jax.numpy as jnp
from jax import lax
from jax.experimental import pallas as pl
from jax.experimental.pallas import tpu as pltpu
from jax.sharding import PartitionSpec as P

MESH = pl.DeviceIdType.MESH
BF = jnp.bfloat16
F32 = jnp.float32

SIN_POLY = (4.442867902973936, -7.30744341898347, 3.594788056349012, -0.7843739717162141)
COS_POLY = (
    1.4142134965673492,
    -6.978850988333631,
    5.739461171609438,
    -1.8835629899115833,
    0.31069819227682083,
)

CHUNK = 256
BLOCK = 1024


def cos_sin(turns):
    r = turns - jnp.round(turns)
    u = r * r
    s = SIN_POLY[-1]
    for a in SIN_POLY[-2::-1]:
        s = s * u + a
    s = s * r
    c = COS_POLY[-1]
    for a in COS_POLY[-2::-1]:
        c = c * u + a
    return 1.0 - s * s, s * c


def dot(a, b):
    return jnp.dot(a, b, preferred_element_type=F32)


def kernel(
    dims,
    codes,
    counts,
    feat_hbm,
    offs,
    waves,
    radial_hbm,
    w_msg,
    w_mix,
    out,
    feat,
    win,
    radial,
    table0,
    table1,
    table2,
    table3,
    pos,
    wop,
    kern,
    acc,
    total,
    core_tx,
    core_rx,
    xy_tx,
    xy_rx,
    z_tx,
    z_rx,
    en,
    halo_s,
    halo_r,
    core_s,
    core_r,
    xy_s,
    xy_r,
    z_s,
    z_r,
    ag_s,
    ag_r,
    fw_s,
    fw_r,
    feat_sem,
    rad_sem,
    out_sem,
):
    nx, ny, zh, zl = dims
    nxy, nz = nx * ny, zh * zl
    cells, atoms, chans = feat.shape
    wave_count = waves.shape[1]
    chunks = wave_count // CHUNK
    piece = CHUNK // nxy
    groups, devs = 2 * zl, nx * ny * zh
    line = cells * devs
    wide = cells + 2

    g = lax.axis_index("grp")
    d = lax.axis_index("dev")
    core, my_zl = lax.rem(g, 2), g // 2
    my_x, my_zh, my_y = lax.rem(d, nx), lax.rem(d // nx, zh), d // (nx * zh)
    my_xy = my_y * nx + my_x
    my_z = my_zh * zl + my_zl
    sibling = (g + 1 - 2 * core, d)

    def xy_peer(step):
        j = lax.rem(my_xy + step, nxy)
        return (g, (j // nx) * (nx * zh) + my_zh * nx + lax.rem(j, nx))

    def z_peer(step):
        j = lax.rem(my_z + step, nz)
        return (lax.rem(j, zl) * 2 + core, my_y * (nx * zh) + (j // zl) * nx + my_x)

    steps = [(-1, 0), (1, 0), (0, -1), (0, 1)]

    def exists(step):
        a, b = step
        return ((g + a >= 0) & (g + a < groups)) & ((d + b >= 0) & (d + b < devs))

    tables = (table0, table1, table2, table3)
    feat_copy = pltpu.make_async_copy(feat_hbm, feat, feat_sem)
    feat_copy.start()
    rad_copy = pltpu.make_async_copy(radial_hbm, radial, rad_sem)
    rad_copy.start()

    barrier = pltpu.get_barrier_semaphore()
    greeted = jnp.int32(1 + (nxy - 1) + (nz - 1))
    for step in steps:
        there = exists(step)
        greeted = greeted + there.astype(jnp.int32)

        @pl.when(there)
        def _():
            pl.semaphore_signal(
                barrier, inc=1, device_id=(g + step[0], d + step[1]), device_id_type=MESH
            )

    def remote(src, dst, send, recv, device):
        return pltpu.make_async_remote_copy(
            src_ref=src, dst_ref=dst, send_sem=send, recv_sem=recv, device_id=device, device_id_type=MESH
        )


    def core_copy(c):
        return remote(core_tx.at[c], core_rx.at[c], core_s.at[c], core_r.at[c], sibling)

    def core_send(c):
        core_tx[c] = acc[c, 1 - core].astype(BF)
        core_copy(c).start()

    def xy_send(c):
        core_copy(c).wait_recv()
        both = acc[c, core] + core_rx[c].astype(F32)
        xy_tx[c] = both.astype(BF)

        @pl.loop(1, nxy)
        def _(step):
            j = lax.rem(my_xy + step, nxy)
            part = pl.ds(pl.multiple_of(j * piece, piece), piece)
            remote(
                xy_tx.at[c, part], xy_rx.at[c, step - 1], xy_s.at[c], xy_r.at[c], xy_peer(step)
            ).start()

    def xy_all(c, send, recv):
        return remote(xy_rx.at[c], xy_rx.at[c], send.at[c], recv.at[c], sibling)

    def z_all(c):
        return remote(z_rx.at[c], z_rx.at[c], z_s.at[c], z_r.at[c], sibling)

    own_part = pl.ds(pl.multiple_of(my_xy * piece, piece), piece)

    def z_send(c):
        xy_all(c, xy_s, xy_r).wait_recv()
        both = xy_tx[c, own_part, :].astype(F32)
        for step in range(nxy - 1):
            both = both + xy_rx[c, step].astype(F32)
        z_tx[c] = both.astype(BF)

        @pl.loop(1, nz, unroll=True)
        def _(step):
            remote(z_tx.at[c], z_rx.at[c, step - 1], z_s.at[c], z_r.at[c], z_peer(step)).start()

    factor_scale = 1.0 / math.sqrt(groups * line * atoms)
    long_scale = 8.0 / math.sqrt(wave_count)

    def ag_send(c):
        z_all(c).wait_recv()
        both = z_tx[c].astype(F32)
        for step in range(nz - 1):
            both = both + z_rx[c, step].astype(F32)
        mixed = dot((both * factor_scale).astype(BF), w_mix[...])
        weight = kern[pl.ds(pl.multiple_of(c * CHUNK + my_xy * piece, piece), piece), :]
        weight = jnp.concatenate([weight] * (chans // 128), axis=1) * long_scale
        en[c, core, own_part, :] = (mixed * weight).astype(BF)

        @pl.loop(1, nxy, unroll=True)
        def _(step):
            mine = en.at[c, core, own_part]
            remote(mine, mine, ag_s.at[c], ag_r.at[c], xy_peer(step)).start()

    def fw_copy(c, which):
        half = en.at[c, which]
        return remote(half, half, fw_s.at[c], fw_r.at[c], sibling)

    def fw_send(c):
        xy_all(c, ag_s, ag_r).wait_recv()
        fw_copy(c, core).start()

    def short_cell(i):
        pairs = radial.shape[1]
        gathered = jnp.zeros((atoms, chans), F32)
        for q in range(0, pairs, 2):
            left, right = codes[q, i], codes[q + 1, i]
            picked = jnp.concatenate(
                [win[code // 3 * wide + i + code % 3] for code in (left, right)], axis=0
            )
            matrix = jnp.concatenate([radial[i, q], radial[i, q + 1]], axis=1)
            gathered = gathered + dot(matrix, picked)
        at = pl.ds(pl.multiple_of(i * atoms, atoms), atoms)
        total[at, :] = dot(gathered.astype(BF), w_msg[...])

    def short_range(lo, hi):
        @pl.loop(lo, hi, step=2)
        def _(first):
            short_cell(first)
            short_cell(first + 1)

    def long_range(c):
        fw_copy(c, 1 - core).wait_recv()

        @pl.loop(0, blocks)
        def _(b):
            total[rows_of(b), :] += dot(tables[c][rows_of(b), :], en[c].reshape(2 * CHUNK, chans))

    def out_copy(b):
        at = pl.ds(b * (block // atoms), block // atoms)
        return pltpu.make_async_copy(feat.at[at], out.at[at], out_sem.at[b])

    def finish(c):
        fw_copy(c, 1 - core).wait_recv()

        @pl.loop(0, blocks)
        def _(b):
            v = total[rows_of(b), :]
            v = v + dot(tables[c][rows_of(b), :], en[c].reshape(2 * CHUNK, chans))
            silu = v / (1.0 + jnp.exp(-v))
            first = b * (block // atoms)
            own = win[pl.ds(wide + 1 + first, block // atoms)].reshape(block, chans).astype(F32)
            result = (own + silu).reshape(block // atoms, atoms, chans)
            for i in range(block // atoms):
                feat[first + i] = jnp.where(rows < counts[first + i], result[i], 0.0).astype(BF)
            out_copy(b).start()

        for b in range(blocks):
            out_copy(b).wait()

    def halo_copy(k):
        _, b = steps[k]
        src = win.at[wide + (cells if b > 0 else 1)]
        dst = win.at[wide + (0 if b > 0 else wide - 1)]
        return remote(src, dst, halo_s.at[k], halo_r.at[k], (g, d + b))

    early = 7 * cells // 8

    def slab_copy(k, part):
        a, _ = steps[k]
        lo, count = (early, cells - early) if part else (0, early)
        which = k + 8 * part
        return remote(
            win.at[pl.ds(wide + 1 + lo, count)],
            win.at[pl.ds((1 - a) * wide + 1 + lo, count)],
            halo_s.at[which],
            halo_r.at[which],
            (g + a, d),
        )

    def start_halo():
        for k in (2, 3):

            @pl.when(exists(steps[k]))
            def _():
                halo_copy(k).start()

        for k in (0, 1):

            @pl.when(exists(steps[k]))
            def _():
                slab_copy(k, 0).start()

            @pl.when(exists(steps[k]) & (core != k))
            def _():
                slab_copy(k, 1).start()

    def start_rest():
        for k in (0, 1):

            @pl.when(exists(steps[k]) & (core == k))
            def _():
                slab_copy(k, 1).start()

    def relay_copy(k, end):
        a, _ = steps[k]
        at = wide - 1 if end else 0
        which = 4 + 2 * k + end
        return remote(
            win.at[wide + at],
            win.at[(1 - a) * wide + at],
            halo_s.at[which],
            halo_r.at[which],
            (g + a, d),
        )

    def both_relays(k, act):
        for end in range(2):
            act(relay_copy(k, end))

    def relay_edges():
        for k in (2, 3):

            @pl.when(exists(steps[5 - k]))
            def _():
                halo_copy(k).wait_recv()

        for k in (0, 1):

            @pl.when(exists(steps[k]))
            def _():
                both_relays(k, lambda copy: copy.start())

    def slabs_arrived():
        for k in (0, 1):

            @pl.when(exists(steps[1 - k]))
            def _():
                slab_copy(k, 0).wait_recv()
                slab_copy(k, 1).wait_recv()

    def relays_arrived():
        for k in (0, 1):

            @pl.when(exists(steps[1 - k]))
            def _():
                both_relays(k, lambda copy: copy.wait_recv())

    @pl.loop(1, nz, unroll=True)
    def _(step):
        pl.semaphore_signal(barrier, inc=1, device_id=z_peer(step), device_id_type=MESH)

    @pl.loop(1, nxy, unroll=True)
    def _(step):
        pl.semaphore_signal(barrier, inc=1, device_id=xy_peer(step), device_id_type=MESH)

    pl.semaphore_signal(barrier, inc=1, device_id=sibling, device_id_type=MESH)

    pos[...] = jnp.zeros_like(pos)
    cell_ids = lax.broadcasted_iota(jnp.int32, (cells, atoms), 0)
    planes = (
        ((d * cells + cell_ids).astype(F32) + offs[0]) / line,
        offs[1],
        (g.astype(F32) + offs[2]) / groups,
    )
    for axis, plane in enumerate(planes):
        for part in range(3):
            rounded = plane.astype(BF).astype(F32)
            plane = plane - rounded
            for i in range(cells):
                pos[8 * part + axis : 8 * part + axis + 1, atoms * i : atoms * (i + 1)] = rounded[
                    i : i + 1
                ]
    waves_f = waves[...].astype(F32)
    wop[...] = jnp.zeros_like(wop)
    for part in range(3):
        wop[8 * part : 8 * part + 3, :] = waves_f

    def first_dims(a, b):
        return lax.dot_general(a, b, (((0,), (0,)), ((), ())), preferred_element_type=F32)

    slots = cells * atoms
    block = min(BLOCK, slots)
    blocks = slots // block

    def rows_of(b):
        return pl.ds(pl.multiple_of(b * block, block), block)

    def make_table(c, step=256):
        turning = wop[:, c * CHUNK : (c + 1) * CHUNK].astype(BF)
        for lo in range(0, slots, step):
            cos, sin = cos_sin(first_dims(pos[:, lo : lo + step].astype(BF), turning))
            tables[c][lo : lo + step, 0:CHUNK] = cos.astype(BF)
            tables[c][lo : lo + step, CHUNK : 2 * CHUNK] = sin.astype(BF)

    def damping():
        square = jnp.sum(waves_f * waves_f, axis=0, keepdims=True)
        ratio = jnp.exp(-square / 128.0) / (1.0 + square / 64.0)
        for b in range(wave_count // 128):
            at = slice(128 * b, 128 * (b + 1))
            kern[at, :] = jnp.broadcast_to(ratio[:, at], (128, 128)).T

    def partial_sums(c):
        mine = win[wide + 1 : wide + 1 + cells].reshape(cells * atoms, chans)
        acc[c] = first_dims(tables[c][...], mine).reshape(2, CHUNK, chans)

    make_table(0)

    rows = lax.broadcasted_iota(jnp.int32, (atoms, chans), 0)
    feat_copy.wait()

    @pl.loop(0, cells)
    def _(i):
        keep = rows < counts[i]
        win[wide + 1 + i] = jnp.where(keep, feat[i].astype(F32), 0.0).astype(BF)

    blank = jnp.zeros((atoms, chans), BF)
    for a in (-1, 1):

        @pl.when(jnp.logical_not(exists((a, 0))))
        def _():
            @pl.loop(0, wide)
            def _(i):
                win[(1 + a) * wide + i] = blank

    for b, end in ((-1, 0), (1, wide - 1)):

        @pl.when(jnp.logical_not(exists((0, b))))
        def _():
            win[wide + end] = blank

    pl.semaphore_wait(barrier, greeted)
    start_halo()
    make_table(1)
    partial_sums(0)
    core_send(0)
    make_table(2)
    partial_sums(1)
    core_send(1)
    xy_send(0)
    make_table(3)
    partial_sums(2)
    core_send(2)
    xy_send(1)
    partial_sums(3)
    core_send(3)
    xy_send(2)
    xy_send(3)
    damping()
    z_send(0)
    z_send(1)
    z_send(2)
    relay_edges()
    z_send(3)
    start_rest()
    rad_copy.wait()
    ag_send(0)
    ag_send(1)
    ag_send(2)
    ag_send(3)
    fw_send(0)
    fw_send(1)
    slabs_arrived()
    relays_arrived()
    short_range(0, cells // 2)
    fw_send(2)
    short_range(cells // 2, 3 * cells // 4)
    fw_send(3)
    short_range(3 * cells // 4, cells)
    long_range(0)
    long_range(1)
    long_range(2)
    finish(3)

    for k in (0, 1):

        @pl.when(exists(steps[k]))
        def _():
            slab_copy(k, 0).wait_send()
            slab_copy(k, 1).wait_send()
            both_relays(k, lambda copy: copy.wait_send())

    for k in (2, 3):

        @pl.when(exists(steps[k]))
        def _():
            halo_copy(k).wait_send()

    for c in range(chunks):
        core_copy(c).wait_send()
        xy_all(c, xy_s, xy_r).wait_send()
        z_all(c).wait_send()
        xy_all(c, ag_s, ag_r).wait_send()
        fw_copy(c, core).wait_send()


def copy_kernel(parts, source, result, held, in_sem, out_sem):
    coming = [pltpu.make_async_copy(source.at[p], held.at[p], in_sem.at[p]) for p in parts]
    going = [pltpu.make_async_copy(held.at[p], result.at[p], out_sem.at[p]) for p in parts]
    for copy in coming:
        copy.start()
    for first, second in zip(coming, going):
        first.wait()
        second.start()
    for copy in going:
        copy.wait()


def copied(array, parts=4):
    split = array.reshape(parts, -1, *array.shape[1:])
    anywhere = pl.BlockSpec(memory_space=pl.ANY)
    return pl.pallas_call(
        functools.partial(copy_kernel, range(parts)),
        out_shape=jax.ShapeDtypeStruct(split.shape, split.dtype),
        in_specs=[anywhere],
        out_specs=anywhere,
        scratch_shapes=[
            pltpu.VMEM(split.shape, split.dtype),
            pltpu.SemaphoreType.DMA((parts,)),
            pltpu.SemaphoreType.DMA((parts,)),
        ],
        compiler_params=pltpu.CompilerParams(vmem_limit_bytes=60000 * 1024),
    )(split).reshape(array.shape)


def body(dims, features, offsets, radial, neighbours, counts, wavevectors, w_msg, w_mix):
    nx, ny, zh, zl = dims
    _, cells, atoms, chans = features.shape
    pairs = neighbours.shape[2]
    wave_count = wavevectors.shape[1]
    chunks = wave_count // CHUNK
    nxy, nz = nx * ny, zh * zl
    piece = CHUNK // nxy
    slots = cells * atoms
    smem = pl.BlockSpec(memory_space=pltpu.SMEM)
    vmem = pl.BlockSpec(memory_space=pltpu.VMEM)
    anywhere = pl.BlockSpec(memory_space=pl.ANY)
    dma = pltpu.SemaphoreType.DMA
    updated = pl.pallas_call(
        functools.partial(kernel, dims),
        out_shape=jax.ShapeDtypeStruct((cells, atoms, chans), BF),
        in_specs=[smem, smem, anywhere, vmem, vmem, anywhere, vmem, vmem],
        out_specs=anywhere,
        scratch_shapes=[
            pltpu.VMEM((cells, atoms, chans), BF),
            pltpu.VMEM((3 * (cells + 2), atoms, chans), BF),
            pltpu.VMEM((cells, pairs, atoms, atoms), BF),
        ]
        + [pltpu.VMEM((slots, 2 * CHUNK), BF)] * chunks
        + [
            pltpu.VMEM((32, slots), F32),
            pltpu.VMEM((32, wave_count), F32),
            pltpu.VMEM((wave_count, 128), F32),
            pltpu.VMEM((chunks, 2, CHUNK, chans), F32),
            pltpu.VMEM((slots, chans), F32),
            pltpu.VMEM((chunks, CHUNK, chans), BF),
            pltpu.VMEM((chunks, CHUNK, chans), BF),
            pltpu.VMEM((chunks, CHUNK, chans), BF),
            pltpu.VMEM((chunks, nxy - 1, piece, chans), BF),
            pltpu.VMEM((chunks, piece, chans), BF),
            pltpu.VMEM((chunks, nz - 1, piece, chans), BF),
            pltpu.VMEM((chunks, 2, CHUNK, chans), BF),
            dma((10,)),
            dma((10,)),
        ]
        + [dma((chunks,))] * 10
        + [dma(())] * 2
        + [dma((max(1, slots // BLOCK),))],
        compiler_params=pltpu.CompilerParams(
            collective_id=0, has_side_effects=True, vmem_limit_bytes=60000 * 1024
        ),
    )(
        neighbours[0].T,
        counts.reshape(cells),
        features[0],
        jnp.transpose(offsets[0], (1, 0, 2)),
        wavevectors,
        radial[0],
        w_msg,
        w_mix,
    )
    return copied(updated)[None]


def solution(mesh):
    groups, devs = mesh.shape["grp"], mesh.shape["dev"]
    nx = 4 if devs >= 32 else 2
    dims = (nx, devs // (2 * nx), 2, groups // 2)
    in_specs = (
        P("grp", "dev", None, None),
        P("grp", "dev", None, None),
        P("grp", "dev", None, None, None),
        P("grp", "dev", None),
        P("grp", "dev"),
        P(),
        P(),
        P(),
    )
    out_specs = P("grp", "dev", None, None)
    return jax.shard_map(
        functools.partial(body, dims),
        mesh=mesh,
        in_specs=in_specs,
        out_specs=out_specs,
        check_vma=False,
    )
```
